128 devices in a mesh: bin: 8 (over y, core), col: 16 (over z, x).
Axes of the slice: x: 4, y: 4, z: 4, core: 2. Of those that a mesh axis runs over, the one named last changes fastest.
Arguments:
- les_source: float32 [128, 106, 16384], P('bin', None, 'col'), may hold values from -6 to 6
- cell_owner: int32 [16384, 1], P('col'), may hold values from 0 to 15; in each aligned block of 1024 rows (0 to 1023, 1024 to 2047, ...) at most 128 rows name the same one
- cell_slot: int32 [16384], P('col'), may hold values from 0 to 127
- pdf_weight: float32 [128, 16384], P('bin', 'col'), may hold values from 0.02 to 0.2
- prior_state: float32 [128, 106, 2048], P('bin', None, 'col'), may hold values from -24 to 24
- dissip: float32 [2048], P('col'), may hold values from 500 to 5000
- react_inverse: float32 [128, 106, 106], P('bin'), may hold values from -0.625 to 0.625
Outputs:
- new_state: float32 [128, 106, 2048], P('bin', None, 'col')
- les_species: float32 [106, 16384], P(None, 'col')
The draws below stay inside these ranges and needn't reach their ends.
Inputs may be any that keep to these rules, and one draw needn't show every extreme that they name: `cell_owner`: among the 1024 cells of one device at most 128 have any one owner, and exactly 128 cells of some device share one owner.
All inputs are finite; a program needn't handle non-finite values.
Results may differ from the reference program's by a relative error of at most 0.00015.
Values sent between devices are 32-bit elements; how exact they have to be, the bound alone decides.
A program may use at most 128 MiB of HBM per device.

```python
import math
import jax
import jax.numpy as jnp
import numpy as np
from jax import lax

S = 106
NB = 128
COL_DEV = 128
LES_DEV = 1024
GROUPS = 16
CAP = 128
COLS = 2048
LES_CELLS = 16384


def with_ends(values, rng, low, high):
    index_at = [jax.random.randint(jax.random.fold_in(rng, axis), (), 0, length) for axis, length in enumerate(values.shape)]
    longest = values.shape.index(max(values.shape))
    next_to = index_at[:longest] + [(index_at[longest] + 1) % values.shape[longest]] + index_at[longest + 1:]
    return values.at[tuple(index_at)].set(low).at[tuple(next_to)].set(high)


def shard_levels(stream_key, dims, pieces, least, high):
    level = 1.0
    for position, blocks in pieces:
        steps = jax.random.uniform(jax.random.fold_in(jax.random.fold_in(stream_key, 6), position), (blocks,), jnp.float32, least / len(pieces), high / len(pieces))
        level = level * jnp.repeat(jnp.exp(steps), dims[position] // blocks).reshape((-1,) + (1,) * (len(dims) - 1 - position))
    return level


def shared_out(stream_key, own, number, rows, amount, top, reach, skew):
    ranking = jax.random.permutation(stream_key, amount)
    heavy_load, usual = load_shares(amount, rows * top, reach, skew, True), load_shares(amount, rows * top, reach, skew, False)
    places = jnp.arange(amount)

    def named(lengths, offset_by):
        used = int((lengths > 0).sum())
        fixed = max(1, used // 4)
        passed = fixed + (places - fixed + offset_by * (used - fixed)) % max(1, amount - fixed)
        return jnp.zeros((amount,), jnp.int32).at[ranking[jnp.where(places < fixed, places, passed)]].set(jnp.asarray(lengths, jnp.int32))

    lengths = jnp.where(number % 4 == 0, named(heavy_load, number // 4), named(usual, number - number // 4 - 1))
    mixed = jax.random.permutation(jax.random.fold_in(own, 3), amount)
    giver, sink = mixed[0:amount // 2 * 2:2], mixed[1:amount // 2 * 2:2]
    slack = jnp.minimum(lengths[giver] - 1, reach - lengths[sink]) // 2
    slack = jnp.where((giver == ranking[0]) | (sink == ranking[0]) | (lengths[sink] == 0), 0, jnp.maximum(slack, 0))
    passed = jax.random.randint(jax.random.fold_in(own, 4), (amount // 2,), 0, 1 << 20) % (slack + 1)
    lengths = lengths.at[giver].add(-passed).at[sink].add(passed)
    items = jnp.searchsorted(jnp.cumsum(lengths), jnp.arange(rows * top), side="right").astype(jnp.int32)
    listing = items.reshape(top, rows).T
    listing = listing[jax.random.permutation(jax.random.fold_in(own, 1), rows)]
    offset_by = jax.random.randint(jax.random.fold_in(own, 2), (rows, 1), 0, top)
    return jnp.take_along_axis(listing, (jnp.arange(top)[None, :] + offset_by) % top, axis=1)


def load_shares(number_of, total, most, slope, full):
    loads = [(1 << 20) // math.isqrt(rank ** slope) + 1 for rank in range(1, number_of + 1)]
    largest = most if full else min(most, max(-(-total // number_of), total * loads[0] // sum(loads)))
    least = 1 if total - largest >= number_of - 1 else 0
    counts, surplus = [largest] + [least] * (number_of - 1), total - largest - least * (number_of - 1)
    while surplus > 0:
        candidates = [i for i in range(1, number_of) if counts[i] < largest] or [i for i in range(1, number_of) if counts[i] < most]
        pool, remaining = sum([loads[i] for i in candidates]), surplus
        for i in candidates:
            more = min(most - counts[i], max(1, remaining * loads[i] // pool), surplus)
            counts[i] = counts[i] + more
            surplus = surplus - more
    return np.array(counts)


def normal_values(rng, extent, spread, reach, split=(), held_as=jnp.bfloat16):
    array = jax.random.normal(rng, extent, jnp.float32) * spread
    if len(split) > 0:
        array = shard_levels(rng, extent, split, -0.22, 0.18) * array
    return jnp.clip(array, min=-reach, max=reach).astype(held_as)


def setup_inputs(seed: int = 0) -> dict:
    arg_keys = jax.random.split(jax.random.key(seed), 8)
    les_source = normal_values(arg_keys[0], (NB, S, LES_CELLS), 1.0, 6.0, ((0, 8), (2, 16)), jnp.float32)
    cell_owner_keys = jax.random.split(jax.random.fold_in(arg_keys[1], 1), LES_CELLS // LES_DEV)
    cell_owner_turns = jax.random.permutation(jax.random.fold_in(arg_keys[1], 3), LES_CELLS // LES_DEV)
    cell_owner = jax.vmap(lambda own, number: shared_out(jax.random.fold_in(arg_keys[1], 2), own, number, LES_DEV, GROUPS, 1, CAP, 2))(cell_owner_keys, cell_owner_turns).reshape((LES_CELLS, 1))
    cell_slot = with_ends(jax.random.randint(arg_keys[2], (LES_CELLS,), 0, COL_DEV), jax.random.fold_in(arg_keys[2], 1), 0, COL_DEV - 1).astype(jnp.int32)
    pdf_weight = jnp.clip(jnp.exp(math.log(0.2) - 2.3025851 * jax.random.uniform(arg_keys[3], (NB, LES_CELLS), jnp.float32) ** shard_levels(arg_keys[3], (NB, LES_CELLS), ((0, 8), (1, 16)), -0.2, 0.2)), 0.02, 0.2)
    prior_state = normal_values(arg_keys[4], (NB, S, COLS), 4.0, 24.0, ((0, 8), (2, 16)), jnp.float32)
    dissip = jnp.clip(jnp.exp(math.log(5000.0) - 2.3025851 * jax.random.uniform(arg_keys[5], (COLS,), jnp.float32) ** shard_levels(arg_keys[5], (COLS,), ((0, 16),), -0.2, 0.2)), 500.0, 5000.0)
    react_inverse = normal_values(arg_keys[6], (NB, S, S), S ** -0.5, 0.625, ((0, 8),), jnp.float32)
    return {"les_source": les_source, "cell_owner": cell_owner, "cell_slot": cell_slot, "pdf_weight": pdf_weight, "prior_state": prior_state, "dissip": dissip, "react_inverse": react_inverse}


def mixing_profile(count):
    centre = (jnp.arange(count, dtype=jnp.float32) + 0.5) / count
    return 4.0 * centre * (1.0 - centre) + 0.05


def reference(les_source, cell_owner, cell_slot, pdf_weight, prior_state, dissip, react_inverse):
    column = (cell_owner[:, 0] * COL_DEV + cell_slot).astype(jnp.int32)
    total_cols = prior_state.shape[2]
    by_cell = jnp.moveaxis(les_source, 2, 0)
    cond_source = jnp.moveaxis(jax.ops.segment_sum(by_cell, column, num_segments=total_cols), 0, 2)
    right_hand_side = prior_state + cond_source
    coeffs = mixing_profile(prior_state.shape[0])[:, None] * dissip[None, :]

    def forward_sweep(running_total, sweep_inputs):
        ratio_earlier, elimination_earlier = running_total
        diffusion, source_term = sweep_inputs
        pivot_current = 1.0 + 2.0 * diffusion - diffusion * ratio_earlier
        ratio_current = diffusion / pivot_current
        elimination_current = source_term / pivot_current[None, :] + ratio_current[None, :] * elimination_earlier
        return (ratio_current, elimination_current), (ratio_current, elimination_current)

    initial_carry = (jnp.zeros((total_cols,), jnp.float32), jnp.zeros(right_hand_side.shape[1:], jnp.float32))
    unused_item, (ratio_values, elimination_terms) = lax.scan(forward_sweep, initial_carry, (coeffs, right_hand_side))

    def backward_sweep(following_entry, sweep_inputs):
        ratio_current, elimination_current = sweep_inputs
        current_entry = elimination_current + ratio_current[None, :] * following_entry
        return current_entry, current_entry

    unused_item, solved_values = lax.scan(backward_sweep, jnp.zeros(right_hand_side.shape[1:], jnp.float32), (ratio_values, elimination_terms), reverse=True)
    new_state = jnp.einsum("ist,itc->isc", react_inverse, solved_values, precision=lax.Precision.HIGHEST)
    at_cells = new_state[:, :, column]
    les_species = jnp.einsum("il,isl->sl", pdf_weight, at_cells, precision=lax.Precision.HIGHEST)
    return new_state, les_species
```

```python
import jax
import jax.numpy as jnp
from jax import lax
from jax.experimental import pallas as pl
from jax.experimental.pallas import tpu as pltpu
from jax.sharding import PartitionSpec as P

highest = lax.Precision.HIGHEST
SIDE = 4
TOP = 56


def split_bf16(value):
    high = value.astype(jnp.bfloat16)
    return high, (value - high.astype(jnp.float32)).astype(jnp.bfloat16)


def scatter_kernel(
    source, relative, prior, right, staged, lhs, onehot, part, relay1, got1, relay2, got2, load_sem, send_sem, recv_sem
):
    bins, species, cells = source.shape
    half = bins // 2
    pad = lhs.shape[0] // 4
    wide = part.shape[-1]
    col = lax.axis_index("col")
    z, x = col // SIDE, lax.rem(col, SIDE)
    x_up, x_down = z * SIDE + lax.rem(x + 1, SIDE), z * SIDE + lax.rem(x + SIDE - 1, SIDE)
    z_up, z_down = lax.rem(z + 1, SIDE) * SIDE + x, lax.rem(z + SIDE - 1, SIDE) * SIDE + x

    def load(step, slot):
        return [
            pltpu.make_async_copy(source.at[step + k * half], staged.at[slot, k], load_sem.at[slot, k]) for k in range(2)
        ]

    for copy in load(0, 0):
        copy.start()
    barrier = pltpu.get_barrier_semaphore()
    for other in (x_up, x_down, z_up, z_down):
        pl.semaphore_signal(barrier, inc=1, device_id={"col": other}, device_id_type=pl.DeviceIdType.MESH)

    lhs[...] = jnp.zeros_like(lhs)
    for n in range(SIDE):
        span = SIDE * wide
        ids = lax.broadcasted_iota(jnp.int32, (cells, span), 1) + n * span
        onehot[:, n * span : (n + 1) * span] = (relative[...] == ids).astype(jnp.float32).astype(jnp.bfloat16)
    pl.semaphore_wait(barrier, 4)

    def copies(b, ways):
        up1, down1, up2, down2 = ways
        low, high = pl.ds(0, TOP), pl.ds(TOP, species - TOP)
        table = [
            (part.at[b, 2, pl.ds(0, 2)], relay1.at[b, 0], up1),
            (part.at[b, 2, pl.ds(2, 2)], relay1.at[b, 1], down1),
            (part.at[b, 1, pl.ds(2, 2)], got1.at[b, 0, pl.ds(2, 2)], up1),
            (part.at[b, 3, pl.ds(0, 2)], got1.at[b, 1, pl.ds(0, 2)], down1),
            (part.at[b, 1, pl.ds(0, 2)], got1.at[b, 0, pl.ds(0, 2)], up1),
            (part.at[b, 3, pl.ds(2, 2)], got1.at[b, 1, pl.ds(2, 2)], down1),
            (part.at[b, 0, 2, low], relay2.at[b, 0], up2),
            (part.at[b, 0, 2, high], relay2.at[b, 1, pl.ds(0, species - TOP)], down2),
            (part.at[b, 0, 1, high], got2.at[b, 0, high], up2),
            (part.at[b, 0, 3, low], got2.at[b, 1, low], down2),
            (part.at[b, 0, 1, low], got2.at[b, 0, low], up2),
            (part.at[b, 0, 3, high], got2.at[b, 1, high], down2),
        ]

        def make(k):
            src, dst, who = table[k]
            return pltpu.make_async_remote_copy(
                src_ref=src,
                dst_ref=dst,
                send_sem=send_sem.at[b, k],
                recv_sem=recv_sem.at[b, k],
                device_id={"col": who},
                device_id_type=pl.DeviceIdType.MESH,
            )

        return make

    ways_of = ((x_up, x_down, z_up, z_down), (z_up, z_down, x_up, x_down))

    def both(step):
        return [copies(step + k * half, ways_of[k]) for k in range(2)]

    def turn(t, carry):
        @pl.when(t < half)
        def produce():
            slot = lax.rem(t, 2)
            for copy in load(t, slot):
                copy.wait()

            @pl.when(t + 1 < half)
            def ahead():
                for copy in load(t + 1, 1 - slot):
                    copy.start()

            for k in range(2):
                high, low = split_bf16(staged[slot, k])
                lhs[k * pad : k * pad + species, :] = high
                lhs[(2 + k) * pad : (2 + k) * pad + species, :] = low
            sends = both(t)
            for dx in (2, 1, 3, 0):
                span = SIDE * wide
                out = jnp.dot(
                    lhs[...], onehot[:, dx * span : (dx + 1) * span], preferred_element_type=jnp.float32
                )
                for k in range(2):
                    total = out[k * pad : k * pad + species] + out[(2 + k) * pad : (2 + k) * pad + species]
                    for dz in range(SIDE):
                        piece = total[:, dz * wide : (dz + 1) * wide]
                        if k == 0:
                            part[t, dx, dz] = piece
                        else:
                            part[t + half, dz, dx] = piece
                if dx == 2:
                    for m in (0, 1):
                        sends[0](m).start()
                if dx == 1:
                    sends[0](2).start()
                if dx == 3:
                    sends[0](3).start()
            for m in range(4):
                sends[1](m).start()

        @pl.when((t >= 1) & (t < half + 1))
        def forward_first():
            for k, flight in enumerate(both(t - 1)):
                b = t - 1 + k * half
                flight(0).wait_recv()
                part[b, 1, 0:2] = part[b, 1, 0:2] + relay1[b, 0]
                flight(4).start()
                flight(1).wait_recv()
                part[b, 3, 2:4] = part[b, 3, 2:4] + relay1[b, 1]
                flight(5).start()

        @pl.when((t >= 2) & (t < half + 2))
        def second_stage():
            for k, flight in enumerate(both(t - 2)):
                b = t - 2 + k * half
                for m in (2, 3, 4, 5):
                    flight(m).wait_recv()
                part[b, 0] = part[b, 0] + got1[b, 0] + got1[b, 1]
                for m in (6, 7, 8, 9):
                    flight(m).start()

        @pl.when((t >= 3) & (t < half + 3))
        def forward_second():
            for k, flight in enumerate(both(t - 3)):
                b = t - 3 + k * half
                flight(6).wait_recv()
                part[b, 0, 1, 0:TOP] = part[b, 0, 1, 0:TOP] + relay2[b, 0]
                flight(10).start()
                flight(7).wait_recv()
                part[b, 0, 3, TOP:species] = part[b, 0, 3, TOP:species] + relay2[b, 1, 0 : species - TOP]
                flight(11).start()

        @pl.when(t >= 4)
        def finish():
            for k, flight in enumerate(both(t - 4)):
                b = t - 4 + k * half
                for m in (8, 9, 10, 11):
                    flight(m).wait_recv()
                right[b] = prior[b] + (part[b, 0, 0] + got2[b, 0] + got2[b, 1])
                for m in range(12):
                    flight(m).wait_send()

        return carry

    lax.fori_loop(0, half + 4, turn, 0)


def scatter_and_reduce(les_source, relative, prior):
    bins, species, cells = les_source.shape
    wide = prior.shape[2]
    pad = -(-species // 16) * 16
    return pl.pallas_call(
        scatter_kernel,
        out_shape=jax.ShapeDtypeStruct(prior.shape, jnp.float32),
        in_specs=[
            pl.BlockSpec(memory_space=pl.ANY),
            pl.BlockSpec(memory_space=pltpu.VMEM),
            pl.BlockSpec(memory_space=pltpu.VMEM),
        ],
        out_specs=pl.BlockSpec(memory_space=pltpu.VMEM),
        scratch_shapes=[
            pltpu.VMEM((2, 2, species, cells), jnp.float32),
            pltpu.VMEM((4 * pad, cells), jnp.bfloat16),
            pltpu.VMEM((cells, SIDE * SIDE * wide), jnp.bfloat16),
            pltpu.VMEM((bins, SIDE, SIDE, species, wide), jnp.float32),
            pltpu.VMEM((bins, 2, 2, species, wide), jnp.float32),
            pltpu.VMEM((bins, 2, SIDE, species, wide), jnp.float32),
            pltpu.VMEM((bins, 2, TOP, wide), jnp.float32),
            pltpu.VMEM((bins, 2, species, wide), jnp.float32),
            pltpu.SemaphoreType.DMA((2, 2)),
            pltpu.SemaphoreType.DMA((bins, 12)),
            pltpu.SemaphoreType.DMA((bins, 12)),
        ],
        compiler_params=pltpu.CompilerParams(collective_id=0, has_side_effects=True, vmem_limit_bytes=58 << 20),
        name="scatter_and_reduce",
    )(les_source, relative, prior)


def prefix(array, axis, combine, identity, reverse):
    count, place = (lax.axis_size(axis), lax.axis_index(axis))
    everything = jax.tree.map(lambda part: lax.all_gather(part, axis), array)
    start = jax.tree.map(
        lambda part, zero: jnp.broadcast_to(jnp.asarray(zero, part.dtype), part.shape),
        array,
        identity,
    )

    def turn(k, before):
        at = count - 1 - k if reverse else k
        reached = at > place if reverse else at < place
        new = combine(before, jax.tree.map(lambda part: part[at], everything))
        return jax.tree.map(lambda a, b: jnp.where(reached, a, b), new, before)

    return lax.fori_loop(0, count, turn, start)


def mixing_profile(count):
    centre = (jnp.arange(count, dtype=jnp.float32) + 0.5) / count
    return 4.0 * centre * (1.0 - centre) + 0.05


def compose_affine(earlier_map, later_map):
    return (earlier_map[0] * later_map[0], later_map[0] * earlier_map[1] + later_map[1])


def pivot_chain(coeffs):

    def advance(ratio_earlier, diffusion):
        pivot_current = 1.0 + 2.0 * diffusion - diffusion * ratio_earlier
        ratio_current = diffusion / pivot_current
        return (ratio_current, (ratio_current, pivot_current))

    unused_item, (ratio_values, pivot_values) = lax.scan(
        advance, jnp.zeros(coeffs.shape[1:], jnp.float32), coeffs
    )
    return (ratio_values, pivot_values)


def running_product(rows, reverse):
    def multiply(before, row):
        new = before * row
        return new, new

    return lax.scan(multiply, jnp.ones(rows.shape[1:], jnp.float32), rows, reverse=reverse)[1]


def bin_solve(right_hand_side, dissip):
    local_bins = right_hand_side.shape[0]
    bin_count = local_bins * lax.axis_size("bin")
    coeffs = mixing_profile(bin_count)[:, None] * dissip[None, :]
    ratios_all, pivots_all = pivot_chain(coeffs)
    first_bin = lax.axis_index("bin") * local_bins
    ratio_values = lax.dynamic_slice_in_dim(ratios_all, first_bin, local_bins, 0)
    pivot_values = lax.dynamic_slice_in_dim(pivots_all, first_bin, local_bins, 0)
    zeroed_plane = jnp.zeros(right_hand_side.shape[1:], jnp.float32)
    identity_line = jnp.ones(right_hand_side.shape[2:], jnp.float32)

    def eliminate_step(previous, sweep_inputs):
        ratio_current, pivot_current, source_term = sweep_inputs
        current_entry = source_term / pivot_current[None, :] + ratio_current[None, :] * previous
        return (current_entry, current_entry)

    unused_item, partial_elimination = lax.scan(
        eliminate_step, zeroed_plane, (ratio_values, pivot_values, right_hand_side)
    )
    growth_factor = running_product(ratio_values, False)
    unused_item, incoming_entry = prefix(
        (growth_factor[-1], partial_elimination[-1]),
        "bin",
        compose_affine,
        (identity_line, zeroed_plane),
        False,
    )
    eliminated_rows = partial_elimination + growth_factor[:, None, :] * incoming_entry[None]

    def substitute(following_entry, sweep_inputs):
        ratio_current, elimination_value = sweep_inputs
        current_entry = elimination_value + ratio_current[None, :] * following_entry
        return (current_entry, current_entry)

    unused_item, partial_back = lax.scan(
        substitute, zeroed_plane, (ratio_values, eliminated_rows), reverse=True
    )
    decay_back = running_product(ratio_values, True)
    unused_item, outgoing = prefix(
        (decay_back[0], partial_back[0]), "bin", compose_affine, (identity_line, zeroed_plane), True
    )
    return partial_back + decay_back[:, None, :] * outgoing[None]


def contract_last(left_mat, right_mat):
    return lax.dot_general(left_mat, right_mat, (((1,), (1,)), ((), ())), precision=highest)


def local(les_source, cell_owner, cell_slot, pdf_weight, prior_state, dissip, react_inverse):
    local_bins, species, cell_num = les_source.shape
    col_local = prior_state.shape[2]
    owner = cell_owner[:, 0]
    column = owner * col_local + cell_slot
    me = lax.axis_index("col")
    ahead_z = (owner // SIDE - me // SIDE) % SIDE
    ahead_x = (owner % SIDE - me % SIDE) % SIDE
    relative = ((ahead_x * SIDE + ahead_z) * col_local + cell_slot)[:, None]
    right_hand_side = scatter_and_reduce(les_source, relative, prior_state)
    solved_values = bin_solve(right_hand_side, dissip)
    new_state = jnp.einsum("ist,itc->isc", react_inverse, solved_values, precision=highest)
    portion = lax.all_gather(new_state, "col", axis=2, tiled=True)
    span_cols = portion.shape[2]
    chosen = (column[:, None] == jnp.arange(span_cols, dtype=jnp.int32)[None, :]).astype(
        jnp.float32
    )
    picked = contract_last(portion.reshape(local_bins * species, span_cols), chosen)
    at_cells = jnp.zeros((local_bins, species, cell_num), jnp.float32) + picked.reshape(
        local_bins, species, cell_num
    )
    partial_species = jnp.einsum("il,isl->sl", pdf_weight, at_cells, precision=highest)
    les_species = lax.psum(partial_species, "bin")
    return (new_state, les_species)


def solution(mesh):
    placed = (
        P("bin", None, "col"),
        P("col", None),
        P("col"),
        P("bin", "col"),
        P("bin", None, "col"),
        P("col"),
        P("bin", None, None),
    )
    return jax.shard_map(
        local,
        mesh=mesh,
        in_specs=placed,
        out_specs=(P("bin", None, "col"), P(None, "col")),
        check_vma=False,
    )
```

```python
import jax
import jax.numpy as jnp
from jax import lax
from jax.experimental import pallas as pl
from jax.experimental.pallas import tpu as pltpu
from jax.sharding import PartitionSpec as P

SIDE = 4
OWNERS = SIDE * SIDE
ROWS = 112
STEPS = 7
MESH = pl.DeviceIdType.MESH


def split_bf16(value):
    high = value.astype(jnp.bfloat16)
    return high, (value - high.astype(jnp.float32)).astype(jnp.bfloat16)


def bf16_where(mask):
    return mask.astype(jnp.float32).astype(jnp.bfloat16)


def step_kernel(
    source, owner, slot, pdf, prior, dissip, react,
    state, les,
    staged, lhs, onehot, packing, before, part, relay1, got1, relay2, got2,
    prior_v, react_v, wide_react, react3, right, ratio, inverse, grown, carried, decayed,
    packed, got_packed, picks, lines, edges, got_edges, ends, got_ends, solved, picked,
    sums, from_twin, relay_b, got_b, total, back, unpacked, gathered,
    load_sem, send_sem, recv_sem, pack_send, pack_recv, edge_send, edge_recv, end_send, end_recv,
    bin_send, bin_recv, back_send, back_recv, all_send, all_recv,
):
    cells = source.shape[1]
    cols = prior.shape[1]
    bins = pdf.shape[0]
    species = prior.shape[0] // bins
    half = prior.shape[0] // 2
    last = half - STEPS * ROWS
    span = SIDE * cols
    padded = solved.shape[1]
    col, bin_ = lax.axis_index("col"), lax.axis_index("bin")
    z, x = col // SIDE, lax.rem(col, SIDE)
    y, core = bin_ // 2, lax.rem(bin_, 2)
    groups = 2 * SIDE

    def col_at(dz, dx):
        return lax.rem(z + dz + SIDE, SIDE) * SIDE + lax.rem(x + dx + SIDE, SIDE)

    def bin_at(dy, other=False):
        return lax.rem(y + dy + SIDE, SIDE) * 2 + (1 - core if other else core)

    x_up, x_down, z_up, z_down = col_at(0, 1), col_at(0, -1), col_at(1, 0), col_at(-1, 0)
    twin = bin_at(0, True)

    def remote(src, dst, sends, recvs, at, axis, who):
        return pltpu.make_async_remote_copy(
            src_ref=src, dst_ref=dst, send_sem=sends.at[at], recv_sem=recvs.at[at],
            device_id={axis: who}, device_id_type=MESH,
        )

    def first_row(c, k):
        return pl.multiple_of(c * ROWS + k * half, 8)

    def load(c, rows, where, k):
        return pltpu.make_async_copy(
            source.at[pl.ds(first_row(c, k), rows)], staged.at[where, k, pl.ds(0, rows)], load_sem.at[where, k]
        )

    def prior_copy():
        return pltpu.make_async_copy(prior, prior_v, load_sem.at[2, 0])

    def react_copy():
        return pltpu.make_async_copy(react, react_v, load_sem.at[2, 1])

    for k in range(2):
        load(0, ROWS, 0, k).start()
    react_copy().start()
    prior_copy().start()
    barrier = pltpu.get_barrier_semaphore()
    for dx in range(SIDE):
        for dz in range(SIDE):
            if dx or dz:
                pl.semaphore_signal(barrier, inc=1, device_id={"col": col_at(dz, dx)}, device_id_type=MESH)
    for d in range(1, groups):
        pl.semaphore_signal(barrier, inc=1, device_id={"bin": lax.rem(bin_ + d, groups)}, device_id_type=MESH)

    ahead = ((owner[...] & (SIDE - 1)) - x) & (SIDE - 1)
    block = ahead * SIDE + (((owner[...] >> 2) - z) & (SIDE - 1))

    def expand(index, target):
        lane = lax.broadcasted_iota(jnp.int32, (128, 128), 1).astype(jnp.float32)
        for q in range(cells // 128):
            tall = jnp.transpose(jnp.broadcast_to(index[:, q * 128 : (q + 1) * 128], (128, 128)))
            for n in range(target.shape[1] // 128):
                target[q * 128 : (q + 1) * 128, n * 128 : (n + 1) * 128] = bf16_where(tall == lane + float(n * 128))

    expand((block * cols + slot[...]).astype(jnp.float32), onehot)
    pl.semaphore_wait(barrier, OWNERS - 1 + groups - 1)

    ways_of = ((x_up, x_down, z_up, z_down), (z_up, z_down, x_up, x_down))

    def flight(c, rows, k):
        b = c + k * (STEPS + 1)
        up1, down1, up2, down2 = ways_of[k]
        every, low, high = pl.ds(0, rows), pl.ds(0, rows // 2), pl.ds(rows // 2, rows // 2)
        first, rest = pl.ds(0, 2), pl.ds(2, 2)
        table = [
            (part.at[b, 2, first, every], relay1.at[b, 0, :, every], up1),
            (part.at[b, 2, rest, every], relay1.at[b, 1, :, every], down1),
            (part.at[b, 1, rest, every], got1.at[b, 0, rest, every], up1),
            (part.at[b, 3, first, every], got1.at[b, 1, first, every], down1),
            (part.at[b, 1, first, every], got1.at[b, 0, first, every], up1),
            (part.at[b, 3, rest, every], got1.at[b, 1, rest, every], down1),
            (part.at[b, 0, 2, low], relay2.at[b, 0, low], up2),
            (part.at[b, 0, 2, high], relay2.at[b, 1, low], down2),
            (part.at[b, 0, 1, high], got2.at[b, 0, high], up2),
            (part.at[b, 0, 3, low], got2.at[b, 1, low], down2),
            (part.at[b, 0, 1, low], got2.at[b, 0, low], up2),
            (part.at[b, 0, 3, high], got2.at[b, 1, high], down2),
        ]

        def make(m):
            src, dst, who = table[m]
            return remote(src, dst, send_sem, recv_sem, (b, m), "col", who)

        return b, make

    def produce(c, rows):
        where = c % 2 if isinstance(c, int) else lax.rem(c, 2)
        for k in range(2):
            load(c, rows, where, k).wait()
        if not isinstance(c, int):

            @pl.when(c + 1 < STEPS)
            def full():
                for k in range(2):
                    load(c + 1, ROWS, 1 - where, k).start()

            @pl.when(c + 1 == STEPS)
            def short():
                for k in range(2):
                    load(STEPS, last, 1 - where, k).start()

        for k in range(2):
            high, low = split_bf16(staged[where, k, 0:rows])
            lhs[k * rows : (k + 1) * rows] = high
            lhs[(2 + k) * rows : (3 + k) * rows] = low
        trips = [flight(c, rows, k) for k in range(2)]
        for dx in (2, 1, 3, 0):
            out = jnp.dot(
                lhs[0 : 4 * rows], onehot[:, dx * span : (dx + 1) * span], preferred_element_type=jnp.float32
            )
            for k in range(2):
                both = out[k * rows : (k + 1) * rows] + out[(2 + k) * rows : (3 + k) * rows]
                for dz in range(SIDE):
                    piece = both[:, dz * cols : (dz + 1) * cols]
                    if k == 0:
                        part[trips[0][0], dx, dz, 0:rows] = piece
                    else:
                        part[trips[1][0], dz, dx, 0:rows] = piece
            for m in {2: (0, 1), 1: (2,), 3: (3,), 0: ()}[dx]:
                trips[0][1](m).start()
        for m in range(4):
            trips[1][1](m).start()

    def forward_first(c, rows):
        for k in range(2):
            b, make = flight(c, rows, k)
            make(0).wait_recv()
            part[b, 1, 0:2, 0:rows] = part[b, 1, 0:2, 0:rows] + relay1[b, 0, :, 0:rows]
            make(4).start()
            make(1).wait_recv()
            part[b, 3, 2:4, 0:rows] = part[b, 3, 2:4, 0:rows] + relay1[b, 1, :, 0:rows]
            make(5).start()

    def second_stage(c, rows):
        for k in range(2):
            b, make = flight(c, rows, k)
            for m in (2, 3, 4, 5):
                make(m).wait_recv()
            part[b, 0, :, 0:rows] = part[b, 0, :, 0:rows] + got1[b, 0, :, 0:rows] + got1[b, 1, :, 0:rows]
            for m in (6, 7, 8, 9):
                make(m).start()

    def forward_second(c, rows):
        low = rows // 2
        for k in range(2):
            b, make = flight(c, rows, k)
            make(6).wait_recv()
            part[b, 0, 1, 0:low] = part[b, 0, 1, 0:low] + relay2[b, 0, 0:low]
            make(10).start()
            make(7).wait_recv()
            part[b, 0, 3, low:rows] = part[b, 0, 3, low:rows] + relay2[b, 1, 0:low]
            make(11).start()

    def finish(c, rows):
        for k in range(2):
            b, make = flight(c, rows, k)
            for m in (8, 9, 10, 11):
                make(m).wait_recv()
            at = pl.ds(first_row(c, k), rows)
            right[at] = prior_v[at] + (part[b, 0, 0, 0:rows] + got2[b, 0, 0:rows] + got2[b, 1, 0:rows])
            for m in range(12):
                make(m).wait_send()

    def pack_copy(n):
        dx, dz = n // SIDE, n % SIDE
        return remote(packed.at[n], got_packed.at[n], pack_send, pack_recv, n, "col", col_at(dz, dx))

    def pack_weights():
        numbers = lax.broadcasted_iota(jnp.int32, (OWNERS, cells), 0)
        mine = numbers == owner[...]
        for q in range(cells // 128):
            rows_ = lax.broadcasted_iota(jnp.int32, (128, cells), 0) + q * 128
            before[q * 128 : (q + 1) * 128] = bf16_where(rows_ < lax.broadcasted_iota(jnp.int32, (128, cells), 1))
        counts = jnp.dot(bf16_where(mine), before[...], preferred_element_type=jnp.float32)
        rank = jnp.sum(jnp.where(mine, counts, 0.0), axis=0, keepdims=True)
        expand((block * 128).astype(jnp.float32) + rank, packing)
        high, low = split_bf16(pdf[...])
        slots = jnp.broadcast_to(slot[...].astype(jnp.float32), (bins, cells)).astype(jnp.bfloat16)
        for n in range(OWNERS):
            at = slice(n * 128, (n + 1) * 128)
            out = jnp.dot(
                jnp.concatenate([high, low, slots], axis=0), packing[:, at], preferred_element_type=jnp.float32
            )
            packed[n, 0:bins] = out[0:bins] + out[bins : 2 * bins]
            packed[n, bins : bins + 8] = out[2 * bins : 2 * bins + 8]
        for n in range(1, OWNERS):
            pack_copy(n).start()

    def take_weights():
        got_packed[0] = packed[0]
        for n in range(1, OWNERS):
            pack_copy(n).wait_recv()
        lane = lax.broadcasted_iota(jnp.int32, (cols, 128), 0).astype(jnp.float32)
        for n in range(OWNERS):
            hit = bf16_where(lane == got_packed[n, bins : bins + 1])
            at = slice(n % 2 * 128, (n % 2 + 1) * 128)
            picks[n // 2, 0:cols, at] = hit
            picks[n // 2, cols : 2 * cols, at] = hit

    def split_react():
        react_copy().wait()
        wide_react[...] = jnp.zeros_like(wide_react)
        wide_react[0 : species * bins, 0:species] = react_v[...]

        def one(i, carry):
            high, low = split_bf16(wide_react[pl.ds(i, ROWS, stride=bins)])
            react3[i, :, 0:128] = high
            react3[i, :, 128:256] = low
            react3[i, :, 256:384] = high
            return carry

        lax.fori_loop(0, bins, one, 0)
        solved[...] = jnp.zeros_like(solved)
        right[species * bins :] = jnp.zeros((right.shape[0] - species * bins, cols), jnp.float32)
        edges[groups - 1] = jnp.zeros_like(edges[groups - 1])
        sums[groups - 1] = jnp.zeros_like(sums[groups - 1])

    every_bin = bins * groups

    def pivots(low, high):
        strength = jnp.broadcast_to(dissip[...], (8, cols))

        def one(i, earlier):
            centre = (i.astype(jnp.float32) + 0.5) / every_bin
            diffusion = strength * (4.0 * centre * (1.0 - centre) + 0.05)
            pivot = 1.0 + 2.0 * diffusion - diffusion * earlier
            new = diffusion / pivot
            ratio[i] = new
            inverse[i] = 1.0 / pivot
            return new

        start = jnp.where(low == 0, jnp.zeros((8, cols), jnp.float32), ratio[jnp.maximum(low - 1, 0)])
        lax.fori_loop(low, high, one, start)

    def factors():
        def block_(m, carry):
            def grow(i, g):
                g = g * ratio[m * bins + i]
                grown[m * bins + i] = g
                return g

            lax.fori_loop(0, bins, grow, jnp.ones((8, cols), jnp.float32))

            def shrink(n, both):
                h, d = both
                i = m * bins + bins - 1 - n
                h = grown[i] + ratio[i] * h
                d = ratio[i] * d
                carried[i] = h
                decayed[i] = d
                return h, d

            lax.fori_loop(0, bins, shrink, (jnp.zeros((8, cols), jnp.float32), jnp.ones((8, cols), jnp.float32)))
            return carry

        lax.fori_loop(0, groups, block_, 0)

    def turn(t, carry):
        produce(t, ROWS)

        @pl.when(t >= 1)
        def _():
            forward_first(t - 1, ROWS)

        @pl.when(t == 1)
        def _():
            pack_weights()

        @pl.when(t == 0)
        def _():
            split_react()

        pivots(t * 20, jnp.minimum(t * 20 + 20, every_bin))

        @pl.when(t >= 2)
        def _():
            second_stage(t - 2, ROWS)

        @pl.when(t >= 3)
        def _():
            forward_second(t - 3, ROWS)

        @pl.when(t == 3)
        def _():
            prior_copy().wait()

        @pl.when(t >= 4)
        def _():
            finish(t - 4, ROWS)

        return carry

    lax.fori_loop(0, STEPS, turn, 0)
    stages = (produce, forward_first, second_stage, forward_second, finish)
    for t in range(STEPS, STEPS + len(stages)):
        for n, stage in enumerate(stages):
            if n <= t and t - n <= STEPS:
                stage(t - n, last if t - n == STEPS else ROWS)
        if t == STEPS:
            factors()
            take_weights()

    base = bin_ * bins
    value = jnp.zeros((ROWS, cols), jnp.float32)
    for i in range(bins):
        value = right[pl.ds(i, ROWS, stride=bins)] * inverse[base + i, 0:1] + ratio[base + i, 0:1] * value
        lines[i] = value
    for j in range(groups - 1):
        edges[j, 0] = value[16 * j : 16 * j + 16]
    value = jnp.zeros((ROWS, cols), jnp.float32)
    for i in reversed(range(bins)):
        value = lines[i] + ratio[base + i, 0:1] * value
        lines[i] = value
    for j in range(groups - 1):
        edges[j, 1] = value[16 * j : 16 * j + 16]

    def edge_copy(d):
        other = lax.rem(bin_ + d, groups)
        return remote(edges.at[other], got_edges.at[d], edge_send, edge_recv, d, "bin", other)

    for d in range(1, groups):
        edge_copy(d).start()
    got_edges[0] = edges[bin_]
    for d in range(1, groups):
        edge_copy(d).wait_recv()
    value = jnp.zeros((16, cols), jnp.float32)
    for m in range(groups):
        ends[m, 0] = value
        value = got_edges[lax.rem(bin_ - m + groups, groups), 0] + decayed[m * bins, 0:1] * value
    value = jnp.zeros((16, cols), jnp.float32)
    for m in reversed(range(groups)):
        ends[m, 1] = value
        value = (
            got_edges[lax.rem(bin_ - m + groups, groups), 1]
            + carried[m * bins, 0:1] * ends[m, 0]
            + decayed[m * bins, 0:1] * value
        )

    def end_copy(d):
        other = lax.rem(bin_ + d, groups)
        return remote(ends.at[other], got_ends.at[bin_], end_send, end_recv, d, "bin", other)

    def end_arrived(d):
        other = lax.rem(bin_ - d + groups, groups)
        return remote(ends.at[other], got_ends.at[other], end_send, end_recv, d, "bin", other)

    for d in range(1, groups):
        end_copy(d).start()
    got_ends[bin_] = ends[bin_]
    for d in range(1, groups):
        end_arrived(d).wait_recv()
    entering = jnp.concatenate([got_ends[j, 0] for j in range(groups - 1)], axis=0)
    leaving = jnp.concatenate([got_ends[j, 1] for j in range(groups - 1)], axis=0)

    for i in range(bins):
        value = lines[i] + carried[base + i, 0:1] * entering + decayed[base + i, 0:1] * leaving
        high, low = split_bf16(value)
        at = i % 2
        solved[at, 0:ROWS] = high
        solved[at, 128 : 128 + ROWS] = high
        solved[at, 256 : 256 + ROWS] = low
        new = jnp.dot(react3[i], solved[at], preferred_element_type=jnp.float32)
        state[pl.ds(i, species, stride=bins)] = new[0:species]
        high, low = split_bf16(new)
        picked[i * ROWS : (i + 1) * ROWS, 0:cols] = high
        picked[i * ROWS : (i + 1) * ROWS, cols : 2 * cols] = low

    def weigh(n, carry):
        out = jnp.dot(picked[...], picks[n], preferred_element_type=jnp.float32)
        for q in range(2):
            acc = jnp.zeros((ROWS, 128), jnp.float32)
            for i in range(bins):
                acc = acc + out[i * ROWS : (i + 1) * ROWS, q * 128 : (q + 1) * 128] * got_packed[2 * n + q, i : i + 1]
            for j in range(groups - 1):
                sums[j, 2 * n + q] = acc[16 * j : 16 * j + 16]
        return carry

    lax.fori_loop(0, OWNERS // 2, weigh, 0)

    def twin_copy(dy):
        return remote(sums.at[bin_at(dy, True)], from_twin.at[dy], bin_send, bin_recv, dy, "bin", twin)

    for dy in (2, 1, 3, 0):
        twin_copy(dy).start()
    y_up, y_down = bin_at(1), bin_at(-1)
    first, rest = pl.ds(0, OWNERS // 2), pl.ds(OWNERS // 2, OWNERS // 2)
    bin_table = [
        (sums.at[bin_at(2), first], relay_b.at[0], y_up),
        (sums.at[bin_at(2), rest], relay_b.at[1], y_down),
        (sums.at[bin_at(1), rest], got_b.at[0, rest], y_up),
        (sums.at[bin_at(3), first], got_b.at[1, first], y_down),
        (sums.at[bin_at(1), first], got_b.at[0, first], y_up),
        (sums.at[bin_at(3), rest], got_b.at[1, rest], y_down),
    ]

    def bin_copy(m):
        src, dst, who = bin_table[m]
        return remote(src, dst, bin_send, bin_recv, SIDE + m, "bin", who)

    for dy, then in ((2, (0, 1)), (1, (2,)), (3, (3,)), (0, ())):
        twin_copy(dy).wait_recv()
        j = bin_at(dy)
        sums[j] = sums[j] + from_twin[dy]
        for m in then:
            bin_copy(m).start()
    middle = OWNERS // 2
    bin_copy(0).wait_recv()
    sums[bin_at(1), 0:middle] = sums[bin_at(1), 0:middle] + relay_b[0]
    bin_copy(4).start()
    bin_copy(1).wait_recv()
    sums[bin_at(3), middle:OWNERS] = sums[bin_at(3), middle:OWNERS] + relay_b[1]
    bin_copy(5).start()
    for m in (2, 3, 4, 5):
        bin_copy(m).wait_recv()
    total[...] = sums[bin_] + got_b[0] + got_b[1]

    def back_copy(n):
        dx, dz = n // SIDE, n % SIDE
        return remote(total.at[n], back.at[n], back_send, back_recv, n, "col", col_at(-dz, -dx))

    for n in range(1, OWNERS):
        back_copy(n).start()
    back[0] = total[0]
    for n in range(OWNERS):
        if n:
            back_copy(n).wait_recv()
        high, low = split_bf16(back[n])
        unpacked[0:16, n * 128 : (n + 1) * 128] = high
        unpacked[16:32, n * 128 : (n + 1) * 128] = low
    out = lax.dot_general(
        unpacked[...], packing[...], (((1,), (1,)), ((), ())), preferred_element_type=jnp.float32
    )
    gathered[bin_] = out[0:16] + out[16:32]

    behind, ahead_, across = bin_at(-1), bin_at(1), bin_at(2)
    top, bottom = pl.ds(0, 8), pl.ds(8, 8)

    def all_copy(m):
        block_of, part_of, who = [
            (bin_, None, y_up),
            (bin_, None, y_down),
            (bin_, None, twin),
            (behind, top, y_up),
            (ahead_, bottom, y_down),
            (behind, None, twin),
            (ahead_, None, twin),
            (across, None, twin),
        ][m]
        ref = gathered.at[block_of] if part_of is None else gathered.at[block_of, part_of]
        return remote(ref, ref, all_send, all_recv, m, "bin", who)

    def all_arrived(m):
        block_of, part_of = [
            (behind, None),
            (ahead_, None),
            (twin, None),
            (across, top),
            (across, bottom),
            (bin_at(-1, True), None),
            (bin_at(1, True), None),
            (bin_at(2, True), None),
        ][m]
        ref = gathered.at[block_of] if part_of is None else gathered.at[block_of, part_of]
        return remote(ref, ref, all_send, all_recv, m, "bin", twin)

    for m in (0, 1, 2):
        all_copy(m).start()
    all_arrived(0).wait_recv()
    all_copy(3).start()
    all_copy(5).start()
    all_arrived(1).wait_recv()
    all_copy(4).start()
    all_copy(6).start()
    all_arrived(3).wait_recv()
    all_arrived(4).wait_recv()
    all_copy(7).start()
    for m in (2, 5, 6, 7):
        all_arrived(m).wait_recv()
    for j in range(groups):
        count = min(16, species - 16 * j)
        if count > 0:
            les[16 * j : 16 * j + count] = gathered[j, 0:count]

    for n in range(1, OWNERS):
        pack_copy(n).wait_send()
        back_copy(n).wait_send()
    for d in range(1, groups):
        edge_copy(d).wait_send()
        end_copy(d).wait_send()
    for dy in range(SIDE):
        twin_copy(dy).wait_send()
    for m in range(6):
        bin_copy(m).wait_send()
    for m in range(8):
        all_copy(m).wait_send()


def local(les_source, cell_owner, cell_slot, pdf_weight, prior_state, dissip, react_inverse):
    bins, species, cells = les_source.shape
    cols = prior_state.shape[2]
    groups = 2 * SIDE
    rows = bins * species
    chunks = 2 * (STEPS + 1)
    f32, bf16 = jnp.float32, jnp.bfloat16

    def by_species(array):
        return jnp.transpose(array, (1, 0, 2)).reshape(rows, array.shape[2])

    vmem, hbm, dma = pl.BlockSpec(memory_space=pltpu.VMEM), pl.BlockSpec(memory_space=pl.ANY), pltpu.SemaphoreType.DMA
    state, les = pl.pallas_call(
        step_kernel,
        out_shape=(jax.ShapeDtypeStruct((rows, cols), f32), jax.ShapeDtypeStruct((species, cells), f32)),
        in_specs=[hbm, vmem, vmem, vmem, hbm, vmem, hbm],
        out_specs=(vmem, vmem),
        scratch_shapes=[
            pltpu.VMEM((2, 2, ROWS, cells), f32),
            pltpu.VMEM((4 * ROWS, cells), bf16),
            pltpu.VMEM((cells, OWNERS * cols), bf16),
            pltpu.VMEM((cells, OWNERS * 128), bf16),
            pltpu.VMEM((cells, cells), bf16),
            pltpu.VMEM((chunks, SIDE, SIDE, ROWS, cols), f32),
            pltpu.VMEM((chunks, 2, 2, ROWS, cols), f32),
            pltpu.VMEM((chunks, 2, SIDE, ROWS, cols), f32),
            pltpu.VMEM((chunks, 2, ROWS // 2, cols), f32),
            pltpu.VMEM((chunks, 2, ROWS, cols), f32),
            pltpu.VMEM((rows, cols), f32),
            pltpu.VMEM((rows, species), f32),
            pltpu.VMEM((ROWS * bins, 128), f32),
            pltpu.VMEM((bins, ROWS, 384), bf16),
            pltpu.VMEM((ROWS * bins, cols), f32),
            pltpu.VMEM((bins * groups, 8, cols), f32),
            pltpu.VMEM((bins * groups, 8, cols), f32),
            pltpu.VMEM((bins * groups, 8, cols), f32),
            pltpu.VMEM((bins * groups, 8, cols), f32),
            pltpu.VMEM((bins * groups, 8, cols), f32),
            pltpu.VMEM((OWNERS, bins + 8, 128), f32),
            pltpu.VMEM((OWNERS, bins + 8, 128), f32),
            pltpu.VMEM((OWNERS // 2, 2 * cols, 256), bf16),
            pltpu.VMEM((bins, ROWS, cols), f32),
            pltpu.VMEM((groups, 2, 16, cols), f32),
            pltpu.VMEM((groups, 2, 16, cols), f32),
            pltpu.VMEM((groups, 2, 16, cols), f32),
            pltpu.VMEM((groups, 2, 16, cols), f32),
            pltpu.VMEM((2, 384, cols), bf16),
            pltpu.VMEM((bins * ROWS, 2 * cols), bf16),
            pltpu.VMEM((groups, OWNERS, 16, 128), f32),
            pltpu.VMEM((SIDE, OWNERS, 16, 128), f32),
            pltpu.VMEM((2, OWNERS // 2, 16, 128), f32),
            pltpu.VMEM((2, OWNERS, 16, 128), f32),
            pltpu.VMEM((OWNERS, 16, 128), f32),
            pltpu.VMEM((OWNERS, 16, 128), f32),
            pltpu.VMEM((32, OWNERS * 128), bf16),
            pltpu.VMEM((groups, 16, cells), f32),
            dma((3, 2)),
            dma((chunks, 12)),
            dma((chunks, 12)),
            dma((OWNERS,)),
            dma((OWNERS,)),
            dma((groups,)),
            dma((groups,)),
            dma((groups,)),
            dma((groups,)),
            dma((SIDE + 6,)),
            dma((SIDE + 6,)),
            dma((OWNERS,)),
            dma((OWNERS,)),
            dma((8,)),
            dma((8,)),
        ],
        compiler_params=pltpu.CompilerParams(collective_id=0, has_side_effects=True, vmem_limit_bytes=63 << 20),
        name="cmc_step",
    )(
        by_species(les_source),
        cell_owner.reshape(1, cells),
        cell_slot.reshape(1, cells),
        pdf_weight,
        by_species(prior_state),
        dissip.reshape(1, cols),
        by_species(react_inverse),
    )
    return jnp.transpose(state.reshape(species, bins, cols), (1, 0, 2)), les


def solution(mesh):
    placed = (
        P("bin", None, "col"),
        P("col", None),
        P("col"),
        P("bin", "col"),
        P("bin", None, "col"),
        P("col"),
        P("bin", None, None),
    )
    return jax.shard_map(
        local,
        mesh=mesh,
        in_specs=placed,
        out_specs=(P("bin", None, "col"), P(None, "col")),
        check_vma=False,
    )
```

```python
import jax
import jax.numpy as jnp
from jax import lax
from jax.experimental import pallas as pl
from jax.experimental.pallas import tpu as pltpu
from jax.sharding import PartitionSpec as P

SIDE = 4
OWNERS = SIDE * SIDE
ROWS = 112
STEPS = 7
MESH = pl.DeviceIdType.MESH


def split_bf16(value):
    high = value.astype(jnp.bfloat16)
    return high, (value - high.astype(jnp.float32)).astype(jnp.bfloat16)


def bf16_where(mask):
    return mask.astype(jnp.float32).astype(jnp.bfloat16)


def step_kernel(
    source, owner, slot, pdf, prior, dissip, react,
    state, les,
    staged, lhs, tall, onehot, packing, before, part, relay1, got1, relay2, got2,
    prior_v, react_v, wide_react, react3, right, ratio, inverse, grown, carried, decayed,
    packed, got_packed, picks, lines, edges, got_edges, ends, got_ends, solved, picked,
    sums, from_twin, relay_b, got_b, total, back, unpacked, gathered,
    load_sem, send_sem, recv_sem, pack_send, pack_recv, edge_send, edge_recv, end_send, end_recv,
    bin_send, bin_recv, back_send, back_recv, all_send, all_recv,
):
    cells = source.shape[1]
    cols = prior.shape[1]
    bins = pdf.shape[0]
    species = prior.shape[0] // bins
    half = prior.shape[0] // 2
    last = half - STEPS * ROWS
    span = SIDE * cols
    padded = solved.shape[1]
    col, bin_ = lax.axis_index("col"), lax.axis_index("bin")
    z, x = col // SIDE, lax.rem(col, SIDE)
    y, core = bin_ // 2, lax.rem(bin_, 2)
    groups = 2 * SIDE

    def col_at(dz, dx):
        return lax.rem(z + dz + SIDE, SIDE) * SIDE + lax.rem(x + dx + SIDE, SIDE)

    def bin_at(dy, other=False):
        return lax.rem(y + dy + SIDE, SIDE) * 2 + (1 - core if other else core)

    x_up, x_down, z_up, z_down = col_at(0, 1), col_at(0, -1), col_at(1, 0), col_at(-1, 0)
    twin = bin_at(0, True)

    def remote(src, dst, sends, recvs, at, axis, who):
        return pltpu.make_async_remote_copy(
            src_ref=src, dst_ref=dst, send_sem=sends.at[at], recv_sem=recvs.at[at],
            device_id={axis: who}, device_id_type=MESH,
        )

    def first_row(c, k):
        return pl.multiple_of(c * ROWS + k * half, 8)

    def load(c, rows, where, k):
        return pltpu.make_async_copy(
            source.at[pl.ds(first_row(c, k), rows)], staged.at[where, k, pl.ds(0, rows)], load_sem.at[where, k]
        )

    def prior_copy():
        return pltpu.make_async_copy(prior, prior_v, load_sem.at[2, 0])

    def react_copy():
        return pltpu.make_async_copy(react, react_v, load_sem.at[2, 1])

    for k in range(2):
        load(0, ROWS, 0, k).start()
    react_copy().start()
    prior_copy().start()
    barrier = pltpu.get_barrier_semaphore()
    for dx in range(SIDE):
        for dz in range(SIDE):
            if dx or dz:
                pl.semaphore_signal(barrier, inc=1, device_id={"col": col_at(dz, dx)}, device_id_type=MESH)
    for d in range(1, groups):
        pl.semaphore_signal(barrier, inc=1, device_id={"bin": lax.rem(bin_ + d, groups)}, device_id_type=MESH)

    ahead = ((owner[...] & (SIDE - 1)) - x) & (SIDE - 1)
    block = ahead * SIDE + (((owner[...] >> 2) - z) & (SIDE - 1))

    relative = (block * cols + slot[...]).astype(jnp.float32)
    for q in range(cells // 128):
        at_q = slice(q * 128, (q + 1) * 128)
        tall[at_q] = jnp.transpose(jnp.broadcast_to(relative[:, at_q], (128, 128)))

    def mark(first, count):
        lane = lax.broadcasted_iota(jnp.int32, (128, 128), 1).astype(jnp.float32)
        for q in range(cells // 128):
            at_q = slice(q * 128, (q + 1) * 128)
            for n in range(first, first + count):
                onehot[at_q, n * 128 : (n + 1) * 128] = bf16_where(tall[at_q] == lane + float(n * 128))

    ways_of = ((x_up, x_down, z_up, z_down), (z_up, z_down, x_up, x_down))

    def flight(c, rows, k):
        b = c + k * (STEPS + 1)
        up1, down1, up2, down2 = ways_of[k]
        every, low, high = pl.ds(0, rows), pl.ds(0, rows // 2), pl.ds(rows // 2, rows // 2)
        first, rest = pl.ds(0, 2), pl.ds(2, 2)
        table = [
            (part.at[b, 2, first, every], relay1.at[b, 0, :, every], up1),
            (part.at[b, 2, rest, every], relay1.at[b, 1, :, every], down1),
            (part.at[b, 1, rest, every], got1.at[b, 0, rest, every], up1),
            (part.at[b, 3, first, every], got1.at[b, 1, first, every], down1),
            (part.at[b, 1, first, every], got1.at[b, 0, first, every], up1),
            (part.at[b, 3, rest, every], got1.at[b, 1, rest, every], down1),
            (part.at[b, 0, 2, low], relay2.at[b, 0, low], up2),
            (part.at[b, 0, 2, high], relay2.at[b, 1, low], down2),
            (part.at[b, 0, 1, high], got2.at[b, 0, high], up2),
            (part.at[b, 0, 3, low], got2.at[b, 1, low], down2),
            (part.at[b, 0, 1, low], got2.at[b, 0, low], up2),
            (part.at[b, 0, 3, high], got2.at[b, 1, high], down2),
        ]

        def make(m):
            src, dst, who = table[m]
            return remote(src, dst, send_sem, recv_sem, (b, m), "col", who)

        return b, make

    def produce(c, rows):
        where = c % 2 if isinstance(c, int) else lax.rem(c, 2)
        for k in range(2):
            load(c, rows, where, k).wait()
        if isinstance(c, int):
            for k in range(2):
                if c + 1 < STEPS:
                    load(c + 1, ROWS, 1 - where, k).start()
        else:

            @pl.when(c + 1 < STEPS)
            def full():
                for k in range(2):
                    load(c + 1, ROWS, 1 - where, k).start()

            @pl.when(c + 1 == STEPS)
            def short():
                for k in range(2):
                    load(STEPS, last, 1 - where, k).start()

        for k in range(2):
            high, low = split_bf16(staged[where, k, 0:rows])
            lhs[k * rows : (k + 1) * rows] = high
            lhs[(2 + k) * rows : (3 + k) * rows] = low
        trips = [flight(c, rows, k) for k in range(2)]
        for dx in (2, 1, 3, 0):
            if isinstance(c, int) and c == 0:
                mark(dx * SIDE, SIDE)
            out = jnp.dot(
                lhs[0 : 4 * rows], onehot[:, dx * span : (dx + 1) * span], preferred_element_type=jnp.float32
            )
            for k in range(2):
                both = out[k * rows : (k + 1) * rows] + out[(2 + k) * rows : (3 + k) * rows]
                for dz in range(SIDE):
                    piece = both[:, dz * cols : (dz + 1) * cols]
                    if k == 0:
                        part[trips[0][0], dx, dz, 0:rows] = piece
                    else:
                        part[trips[1][0], dz, dx, 0:rows] = piece
            if isinstance(c, int) and c == 0 and dx == 2:
                pl.semaphore_wait(barrier, OWNERS - 1 + groups - 1)
            for m in {2: (0, 1), 1: (2,), 3: (3,), 0: ()}[dx]:
                trips[0][1](m).start()
        for m in range(4):
            trips[1][1](m).start()

    def forward_first(c, rows):
        for k in range(2):
            b, make = flight(c, rows, k)
            make(0).wait_recv()
            part[b, 1, 0:2, 0:rows] = part[b, 1, 0:2, 0:rows] + relay1[b, 0, :, 0:rows]
            make(4).start()
            make(1).wait_recv()
            part[b, 3, 2:4, 0:rows] = part[b, 3, 2:4, 0:rows] + relay1[b, 1, :, 0:rows]
            make(5).start()

    def second_stage(c, rows):
        for k in range(2):
            b, make = flight(c, rows, k)
            for m in (2, 3, 4, 5):
                make(m).wait_recv()
            part[b, 0, :, 0:rows] = part[b, 0, :, 0:rows] + got1[b, 0, :, 0:rows] + got1[b, 1, :, 0:rows]
            for m in (6, 7, 8, 9):
                make(m).start()

    def forward_second(c, rows):
        low = rows // 2
        for k in range(2):
            b, make = flight(c, rows, k)
            make(6).wait_recv()
            part[b, 0, 1, 0:low] = part[b, 0, 1, 0:low] + relay2[b, 0, 0:low]
            make(10).start()
            make(7).wait_recv()
            part[b, 0, 3, low:rows] = part[b, 0, 3, low:rows] + relay2[b, 1, 0:low]
            make(11).start()

    def finish(c, rows):
        for k in range(2):
            b, make = flight(c, rows, k)
            for m in (8, 9, 10, 11):
                make(m).wait_recv()
            at = pl.ds(first_row(c, k), rows)
            right[at] = prior_v[at] + (part[b, 0, 0, 0:rows] + got2[b, 0, 0:rows] + got2[b, 1, 0:rows])
            for m in range(12):
                make(m).wait_send()

    def pack_copy(n):
        dx, dz = n // SIDE, n % SIDE
        return remote(packed.at[n], got_packed.at[n], pack_send, pack_recv, n, "col", col_at(dz, dx))

    def pack_weights():
        numbers = lax.broadcasted_iota(jnp.int32, (OWNERS, cells), 0)
        mine = numbers == owner[...]
        for q in range(cells // 128):
            rows_ = lax.broadcasted_iota(jnp.int32, (128, cells), 0) + q * 128
            before[q * 128 : (q + 1) * 128] = bf16_where(rows_ < lax.broadcasted_iota(jnp.int32, (128, cells), 1))
        counts = jnp.dot(bf16_where(mine), before[...], preferred_element_type=jnp.float32)
        rank = jnp.sum(jnp.where(mine, counts, 0.0), axis=0, keepdims=True)
        place = (block * 128).astype(jnp.float32) + rank
        for n in range(OWNERS):
            packing[n * 128 : (n + 1) * 128] = bf16_where(
                lax.broadcasted_iota(jnp.int32, (128, cells), 0).astype(jnp.float32) + float(n * 128) == place
            )
        high, low = split_bf16(pdf[...])
        slots = jnp.broadcast_to(slot[...].astype(jnp.float32), (bins, cells)).astype(jnp.bfloat16)
        for n in range(OWNERS):
            at = slice(n * 128, (n + 1) * 128)
            out = lax.dot_general(
                jnp.concatenate([high, low, slots], axis=0), packing[at], (((1,), (1,)), ((), ())),
                preferred_element_type=jnp.float32,
            )
            packed[n, 0:bins] = out[0:bins] + out[bins : 2 * bins]
            packed[n, bins : bins + 8] = out[2 * bins : 2 * bins + 8]
        for n in range(1, OWNERS):
            pack_copy(n).start()

    def take_weights():
        got_packed[0] = packed[0]
        for n in range(1, OWNERS):
            pack_copy(n).wait_recv()
        lane = lax.broadcasted_iota(jnp.int32, (cols, 128), 0).astype(jnp.float32)
        for n in range(OWNERS):
            hit = bf16_where(lane == got_packed[n, bins : bins + 1])
            at = slice(n % 2 * 128, (n % 2 + 1) * 128)
            picks[n // 2, 0:cols, at] = hit
            picks[n // 2, cols : 2 * cols, at] = hit

    def split_react():
        react_copy().wait()
        wide_react[...] = jnp.zeros_like(wide_react)
        wide_react[0 : species * bins, 0:species] = react_v[...]

        def one(i, carry):
            high, low = split_bf16(wide_react[pl.ds(i, ROWS, stride=bins)])
            react3[i, :, 0:128] = high
            react3[i, :, 128:256] = low
            react3[i, :, 256:384] = high
            return carry

        lax.fori_loop(0, bins, one, 0)
        solved[...] = jnp.zeros_like(solved)
        right[species * bins :] = jnp.zeros((right.shape[0] - species * bins, cols), jnp.float32)
        edges[groups - 1] = jnp.zeros_like(edges[groups - 1])
        sums[groups - 1] = jnp.zeros_like(sums[groups - 1])

    every_bin = bins * groups

    def pivots(low, high):
        strength = jnp.broadcast_to(dissip[...], (8, cols))

        def one(i, earlier):
            centre = (i.astype(jnp.float32) + 0.5) / every_bin
            diffusion = strength * (4.0 * centre * (1.0 - centre) + 0.05)
            pivot = 1.0 + 2.0 * diffusion - diffusion * earlier
            new = diffusion / pivot
            ratio[i] = new
            inverse[i] = 1.0 / pivot
            return new

        start = jnp.where(low == 0, jnp.zeros((8, cols), jnp.float32), ratio[jnp.maximum(low - 1, 0)])
        lax.fori_loop(low, high, one, start)

    def factors():
        def block_(m, carry):
            def grow(i, g):
                g = g * ratio[m * bins + i]
                grown[m * bins + i] = g
                return g

            lax.fori_loop(0, bins, grow, jnp.ones((8, cols), jnp.float32))

            def shrink(n, both):
                h, d = both
                i = m * bins + bins - 1 - n
                h = grown[i] + ratio[i] * h
                d = ratio[i] * d
                carried[i] = h
                decayed[i] = d
                return h, d

            lax.fori_loop(0, bins, shrink, (jnp.zeros((8, cols), jnp.float32), jnp.ones((8, cols), jnp.float32)))
            return carry

        lax.fori_loop(0, groups, block_, 0)

    def turn(t, carry):
        produce(t, ROWS)
        forward_first(t - 1, ROWS)

        @pl.when(t == 1)
        def _():
            pack_weights()

        pivots((t - 1) * 22, jnp.minimum(t * 22, every_bin))

        @pl.when(t >= 2)
        def _():
            second_stage(t - 2, ROWS)

        @pl.when(t >= 3)
        def _():
            forward_second(t - 3, ROWS)

        @pl.when(t == 3)
        def _():
            prior_copy().wait()

        @pl.when(t >= 4)
        def _():
            finish(t - 4, ROWS)

        return carry

    produce(0, ROWS)
    split_react()
    lax.fori_loop(1, STEPS, turn, 0)
    stages = (produce, forward_first, second_stage, forward_second, finish)
    for t in range(STEPS, STEPS + len(stages)):
        for n, stage in enumerate(stages):
            if n <= t and t - n <= STEPS:
                stage(t - n, last if t - n == STEPS else ROWS)
        if t == STEPS:
            factors()
            take_weights()

    base = bin_ * bins
    value = jnp.zeros((ROWS, cols), jnp.float32)
    for i in range(bins):
        value = right[pl.ds(i, ROWS, stride=bins)] * inverse[base + i, 0:1] + ratio[base + i, 0:1] * value
        lines[i] = value
    for j in range(groups - 1):
        edges[j, 0] = value[16 * j : 16 * j + 16]
    value = jnp.zeros((ROWS, cols), jnp.float32)
    for i in reversed(range(bins)):
        value = lines[i] + ratio[base + i, 0:1] * value
        lines[i] = value
    for j in range(groups - 1):
        edges[j, 1] = value[16 * j : 16 * j + 16]

    def edge_copy(d):
        other = lax.rem(bin_ + d, groups)
        return remote(edges.at[other], got_edges.at[d], edge_send, edge_recv, d, "bin", other)

    for d in range(1, groups):
        edge_copy(d).start()
    got_edges[0] = edges[bin_]
    for d in range(1, groups):
        edge_copy(d).wait_recv()
    value = jnp.zeros((16, cols), jnp.float32)
    for m in range(groups):
        ends[m, 0] = value
        value = got_edges[lax.rem(bin_ - m + groups, groups), 0] + decayed[m * bins, 0:1] * value
    value = jnp.zeros((16, cols), jnp.float32)
    for m in reversed(range(groups)):
        ends[m, 1] = value
        value = (
            got_edges[lax.rem(bin_ - m + groups, groups), 1]
            + carried[m * bins, 0:1] * ends[m, 0]
            + decayed[m * bins, 0:1] * value
        )

    def end_copy(d):
        other = lax.rem(bin_ + d, groups)
        return remote(ends.at[other], got_ends.at[bin_], end_send, end_recv, d, "bin", other)

    def end_arrived(d):
        other = lax.rem(bin_ - d + groups, groups)
        return remote(ends.at[other], got_ends.at[other], end_send, end_recv, d, "bin", other)

    for d in range(1, groups):
        end_copy(d).start()
    got_ends[bin_] = ends[bin_]
    for d in range(1, groups):
        end_arrived(d).wait_recv()
    entering = jnp.concatenate([got_ends[j, 0] for j in range(groups - 1)], axis=0)
    leaving = jnp.concatenate([got_ends[j, 1] for j in range(groups - 1)], axis=0)

    for i in range(bins):
        value = lines[i] + carried[base + i, 0:1] * entering + decayed[base + i, 0:1] * leaving
        high, low = split_bf16(value)
        at = i % 2
        solved[at, 0:ROWS] = high
        solved[at, 128 : 128 + ROWS] = high
        solved[at, 256 : 256 + ROWS] = low
        new = jnp.dot(react3[i], solved[at], preferred_element_type=jnp.float32)
        state[pl.ds(i, species, stride=bins)] = new[0:species]
        high, low = split_bf16(new)
        picked[i * ROWS : (i + 1) * ROWS, 0:cols] = high
        picked[i * ROWS : (i + 1) * ROWS, cols : 2 * cols] = low

    def weigh(n, carry):
        out = jnp.dot(picked[...], picks[n], preferred_element_type=jnp.float32)
        for q in range(2):
            acc = jnp.zeros((ROWS, 128), jnp.float32)
            for i in range(bins):
                acc = acc + out[i * ROWS : (i + 1) * ROWS, q * 128 : (q + 1) * 128] * got_packed[2 * n + q, i : i + 1]
            for j in range(groups - 1):
                sums[j, 2 * n + q] = acc[16 * j : 16 * j + 16]
        return carry

    middle = OWNERS // 2
    parts = (pl.ds(0, middle), pl.ds(middle, middle))

    def twin_copy(dy, h):
        return remote(
            sums.at[bin_at(dy, True), parts[h]], from_twin.at[dy, parts[h]], bin_send, bin_recv, 2 * dy + h, "bin", twin
        )

    y_up, y_down = bin_at(1), bin_at(-1)
    first, rest = parts
    bin_table = [
        (sums.at[bin_at(2), first], relay_b.at[0], y_up),
        (sums.at[bin_at(2), rest], relay_b.at[1], y_down),
        (sums.at[bin_at(1), rest], got_b.at[0, rest], y_up),
        (sums.at[bin_at(3), first], got_b.at[1, first], y_down),
        (sums.at[bin_at(1), first], got_b.at[0, first], y_up),
        (sums.at[bin_at(3), rest], got_b.at[1, rest], y_down),
    ]

    def bin_copy(m):
        src, dst, who = bin_table[m]
        return remote(src, dst, bin_send, bin_recv, 2 * SIDE + m, "bin", who)

    def join_twin(h):
        for dy, m in ((2, h), (3, 3) if h == 0 else (1, 2), (1, None) if h == 0 else (3, None), (0, None)):
            twin_copy(dy, h).wait_recv()
            j = bin_at(dy)
            at = slice(h * middle, (h + 1) * middle)
            sums[j, at] = sums[j, at] + from_twin[dy, at]
            if m is not None:
                bin_copy(m).start()

    lax.fori_loop(0, 4, weigh, 0)
    for dy in (2, 3, 1, 0):
        twin_copy(dy, 0).start()
    lax.fori_loop(4, 6, weigh, 0)
    join_twin(0)
    lax.fori_loop(6, 8, weigh, 0)
    for dy in (2, 1, 3, 0):
        twin_copy(dy, 1).start()
    bin_copy(0).wait_recv()
    sums[bin_at(1), 0:middle] = sums[bin_at(1), 0:middle] + relay_b[0]
    bin_copy(4).start()
    join_twin(1)
    bin_copy(1).wait_recv()
    sums[bin_at(3), middle:OWNERS] = sums[bin_at(3), middle:OWNERS] + relay_b[1]
    bin_copy(5).start()
    for m in (2, 3, 4, 5):
        bin_copy(m).wait_recv()
    total[...] = sums[bin_] + got_b[0] + got_b[1]

    def back_copy(n):
        dx, dz = n // SIDE, n % SIDE
        return remote(total.at[n], back.at[n], back_send, back_recv, n, "col", col_at(-dz, -dx))

    for n in range(1, OWNERS):
        back_copy(n).start()
    back[0] = total[0]
    mine_sum = jnp.zeros((32, cells), jnp.float32)
    for dx in range(SIDE):
        for dz in range(SIDE):
            n = dx * SIDE + dz
            if n:
                back_copy(n).wait_recv()
            high, low = split_bf16(back[n])
            unpacked[dx, 0:16, dz * 128 : (dz + 1) * 128] = high
            unpacked[dx, 16:32, dz * 128 : (dz + 1) * 128] = low
        mine_sum = mine_sum + jnp.dot(
            unpacked[dx], packing[dx * SIDE * 128 : (dx + 1) * SIDE * 128], preferred_element_type=jnp.float32
        )
    gathered[bin_] = mine_sum[0:16] + mine_sum[16:32]

    behind, ahead_, across = bin_at(-1), bin_at(1), bin_at(2)
    top, bottom = pl.ds(0, 8), pl.ds(8, 8)

    def all_copy(m):
        block_of, part_of, who = [
            (bin_, None, y_up),
            (bin_, None, y_down),
            (bin_, None, twin),
            (behind, top, y_up),
            (ahead_, bottom, y_down),
            (behind, None, twin),
            (ahead_, None, twin),
            (across, None, twin),
        ][m]
        ref = gathered.at[block_of] if part_of is None else gathered.at[block_of, part_of]
        return remote(ref, ref, all_send, all_recv, m, "bin", who)

    def all_arrived(m):
        block_of, part_of = [
            (behind, None),
            (ahead_, None),
            (twin, None),
            (across, top),
            (across, bottom),
            (bin_at(-1, True), None),
            (bin_at(1, True), None),
            (bin_at(2, True), None),
        ][m]
        ref = gathered.at[block_of] if part_of is None else gathered.at[block_of, part_of]
        return remote(ref, ref, all_send, all_recv, m, "bin", twin)

    for m in (0, 1, 2):
        all_copy(m).start()
    all_arrived(0).wait_recv()
    all_copy(3).start()
    all_copy(5).start()
    all_arrived(1).wait_recv()
    all_copy(4).start()
    all_copy(6).start()
    all_arrived(3).wait_recv()
    all_arrived(4).wait_recv()
    all_copy(7).start()
    for m in (2, 5, 6, 7):
        all_arrived(m).wait_recv()
    for j in range(groups):
        count = min(16, species - 16 * j)
        if count > 0:
            les[16 * j : 16 * j + count] = gathered[j, 0:count]

    for n in range(1, OWNERS):
        pack_copy(n).wait_send()
        back_copy(n).wait_send()
    for d in range(1, groups):
        edge_copy(d).wait_send()
        end_copy(d).wait_send()
    for dy in range(SIDE):
        for h in range(2):
            twin_copy(dy, h).wait_send()
    for m in range(6):
        bin_copy(m).wait_send()
    for m in range(8):
        all_copy(m).wait_send()


def local(les_source, cell_owner, cell_slot, pdf_weight, prior_state, dissip, react_inverse):
    bins, species, cells = les_source.shape
    cols = prior_state.shape[2]
    groups = 2 * SIDE
    rows = bins * species
    chunks = 2 * (STEPS + 1)
    f32, bf16 = jnp.float32, jnp.bfloat16

    def by_species(array):
        return jnp.transpose(array, (1, 0, 2)).reshape(rows, array.shape[2])

    vmem, hbm, dma = pl.BlockSpec(memory_space=pltpu.VMEM), pl.BlockSpec(memory_space=pl.ANY), pltpu.SemaphoreType.DMA
    state, les = pl.pallas_call(
        step_kernel,
        out_shape=(jax.ShapeDtypeStruct((rows, cols), f32), jax.ShapeDtypeStruct((species, cells), f32)),
        in_specs=[hbm, vmem, vmem, vmem, hbm, vmem, hbm],
        out_specs=(vmem, vmem),
        scratch_shapes=[
            pltpu.VMEM((2, 2, ROWS, cells), f32),
            pltpu.VMEM((4 * ROWS, cells), bf16),
            pltpu.VMEM((cells, 128), f32),
            pltpu.VMEM((cells, OWNERS * cols), bf16),
            pltpu.VMEM((OWNERS * 128, cells), bf16),
            pltpu.VMEM((cells, cells), bf16),
            pltpu.VMEM((chunks, SIDE, SIDE, ROWS, cols), f32),
            pltpu.VMEM((chunks, 2, 2, ROWS, cols), f32),
            pltpu.VMEM((chunks, 2, SIDE, ROWS, cols), f32),
            pltpu.VMEM((chunks, 2, ROWS // 2, cols), f32),
            pltpu.VMEM((chunks, 2, ROWS, cols), f32),
            pltpu.VMEM((rows, cols), f32),
            pltpu.VMEM((rows, species), f32),
            pltpu.VMEM((ROWS * bins, 128), f32),
            pltpu.VMEM((bins, ROWS, 384), bf16),
            pltpu.VMEM((ROWS * bins, cols), f32),
            pltpu.VMEM((bins * groups, 8, cols), f32),
            pltpu.VMEM((bins * groups, 8, cols), f32),
            pltpu.VMEM((bins * groups, 8, cols), f32),
            pltpu.VMEM((bins * groups, 8, cols), f32),
            pltpu.VMEM((bins * groups, 8, cols), f32),
            pltpu.VMEM((OWNERS, bins + 8, 128), f32),
            pltpu.VMEM((OWNERS, bins + 8, 128), f32),
            pltpu.VMEM((OWNERS // 2, 2 * cols, 256), bf16),
            pltpu.VMEM((bins, ROWS, cols), f32),
            pltpu.VMEM((groups, 2, 16, cols), f32),
            pltpu.VMEM((groups, 2, 16, cols), f32),
            pltpu.VMEM((groups, 2, 16, cols), f32),
            pltpu.VMEM((groups, 2, 16, cols), f32),
            pltpu.VMEM((2, 384, cols), bf16),
            pltpu.VMEM((bins * ROWS, 2 * cols), bf16),
            pltpu.VMEM((groups, OWNERS, 16, 128), f32),
            pltpu.VMEM((SIDE, OWNERS, 16, 128), f32),
            pltpu.VMEM((2, OWNERS // 2, 16, 128), f32),
            pltpu.VMEM((2, OWNERS, 16, 128), f32),
            pltpu.VMEM((OWNERS, 16, 128), f32),
            pltpu.VMEM((OWNERS, 16, 128), f32),
            pltpu.VMEM((SIDE, 32, SIDE * 128), bf16),
            pltpu.VMEM((groups, 16, cells), f32),
            dma((3, 2)),
            dma((chunks, 12)),
            dma((chunks, 12)),
            dma((OWNERS,)),
            dma((OWNERS,)),
            dma((groups,)),
            dma((groups,)),
            dma((groups,)),
            dma((groups,)),
            dma((2 * SIDE + 6,)),
            dma((2 * SIDE + 6,)),
            dma((OWNERS,)),
            dma((OWNERS,)),
            dma((8,)),
            dma((8,)),
        ],
        compiler_params=pltpu.CompilerParams(collective_id=0, has_side_effects=True, vmem_limit_bytes=63 << 20),
        name="cmc_step",
    )(
        by_species(les_source),
        cell_owner.reshape(1, cells),
        cell_slot.reshape(1, cells),
        pdf_weight,
        by_species(prior_state),
        dissip.reshape(1, cols),
        by_species(react_inverse),
    )
    return jnp.transpose(state.reshape(species, bins, cols), (1, 0, 2)), les


def solution(mesh):
    placed = (
        P("bin", None, "col"),
        P("col", None),
        P("col"),
        P("bin", "col"),
        P("bin", None, "col"),
        P("col"),
        P("bin", None, None),
    )
    return jax.shard_map(
        local,
        mesh=mesh,
        in_specs=placed,
        out_specs=(P("bin", None, "col"), P(None, "col")),
        check_vma=False,
    )
```

```python
import jax
import jax.numpy as jnp
from jax import lax
from jax.experimental import pallas as pl
from jax.experimental.pallas import tpu as pltpu
from jax.sharding import PartitionSpec as P

SIDE = 4
OWNERS = SIDE * SIDE
ROWS = 112
STEPS = 7
MESH = pl.DeviceIdType.MESH


def split_bf16(value):
    high = value.astype(jnp.bfloat16)
    return high, (value - high.astype(jnp.float32)).astype(jnp.bfloat16)


def bf16_where(mask):
    return mask.astype(jnp.float32).astype(jnp.bfloat16)


def step_kernel(
    source, owner, slot, pdf, prior, dissip, react,
    state, les,
    staged, lhs, tall, onehot, packing, before, part, relay1, got1, relay2, got2,
    prior_v, react_v, wide_react, react3, right, ratio, inverse, grown, carried, decayed,
    packed, got_packed, picks, lines, edges, got_edges, ends, got_ends, solved, picked,
    sums, from_twin, relay_b, got_b, total, back, unpacked, gathered,
    load_sem, send_sem, recv_sem, pack_send, pack_recv, edge_send, edge_recv, end_send, end_recv,
    bin_send, bin_recv, back_send, back_recv, all_send, all_recv,
):
    cells = source.shape[1]
    cols = prior.shape[1]
    bins = pdf.shape[0]
    species = prior.shape[0] // bins
    half = prior.shape[0] // 2
    last = half - STEPS * ROWS
    span = SIDE * cols
    padded = solved.shape[1]
    col, bin_ = lax.axis_index("col"), lax.axis_index("bin")
    z, x = col // SIDE, lax.rem(col, SIDE)
    y, core = bin_ // 2, lax.rem(bin_, 2)
    groups = 2 * SIDE

    def col_at(dz, dx):
        return lax.rem(z + dz + SIDE, SIDE) * SIDE + lax.rem(x + dx + SIDE, SIDE)

    def bin_at(dy, other=False):
        return lax.rem(y + dy + SIDE, SIDE) * 2 + (1 - core if other else core)

    x_up, x_down, z_up, z_down = col_at(0, 1), col_at(0, -1), col_at(1, 0), col_at(-1, 0)
    twin = bin_at(0, True)

    def remote(src, dst, sends, recvs, at, axis, who):
        return pltpu.make_async_remote_copy(
            src_ref=src, dst_ref=dst, send_sem=sends.at[at], recv_sem=recvs.at[at],
            device_id={axis: who}, device_id_type=MESH,
        )

    def first_row(c, k):
        return pl.multiple_of(c * ROWS + k * half, 8)

    def load(c, rows, where, k):
        return pltpu.make_async_copy(
            source.at[pl.ds(first_row(c, k), rows)], staged.at[where, k, pl.ds(0, rows)], load_sem.at[where, k]
        )

    def prior_copy():
        return pltpu.make_async_copy(prior, prior_v, load_sem.at[2, 0])

    def react_copy():
        return pltpu.make_async_copy(react, react_v, load_sem.at[2, 1])

    for k in range(2):
        load(0, ROWS, 0, k).start()
    react_copy().start()
    prior_copy().start()
    barrier = pltpu.get_barrier_semaphore()
    for dx in range(SIDE):
        for dz in range(SIDE):
            if dx or dz:
                pl.semaphore_signal(barrier, inc=1, device_id={"col": col_at(dz, dx)}, device_id_type=MESH)
    for d in range(1, groups):
        pl.semaphore_signal(barrier, inc=1, device_id={"bin": lax.rem(bin_ + d, groups)}, device_id_type=MESH)

    ahead = ((owner[...] & (SIDE - 1)) - x) & (SIDE - 1)
    block = ahead * SIDE + (((owner[...] >> 2) - z) & (SIDE - 1))

    relative = (block * cols + slot[...]).astype(jnp.float32)
    for q in range(cells // 128):
        at_q = slice(q * 128, (q + 1) * 128)
        tall[at_q] = jnp.transpose(jnp.broadcast_to(relative[:, at_q], (128, 128)))

    def mark(first, count):
        lane = lax.broadcasted_iota(jnp.int32, (128, 128), 1).astype(jnp.float32)
        for q in range(cells // 128):
            at_q = slice(q * 128, (q + 1) * 128)
            for n in range(first, first + count):
                onehot[at_q, n * 128 : (n + 1) * 128] = bf16_where(tall[at_q] == lane + float(n * 128))

    ways_of = ((x_up, x_down, z_up, z_down), (z_up, z_down, x_up, x_down))

    def flight(c, rows, k):
        b = c + k * (STEPS + 1)
        up1, down1, up2, down2 = ways_of[k]
        every, low, high = pl.ds(0, rows), pl.ds(0, rows // 2), pl.ds(rows // 2, rows // 2)
        first, rest = pl.ds(0, 2), pl.ds(2, 2)
        table = [
            (part.at[b, 2, first, every], relay1.at[b, 0, :, every], up1),
            (part.at[b, 2, rest, every], relay1.at[b, 1, :, every], down1),
            (part.at[b, 1, rest, every], got1.at[b, 0, rest, every], up1),
            (part.at[b, 3, first, every], got1.at[b, 1, first, every], down1),
            (part.at[b, 1, first, every], got1.at[b, 0, first, every], up1),
            (part.at[b, 3, rest, every], got1.at[b, 1, rest, every], down1),
            (part.at[b, 0, 2, low], relay2.at[b, 0, low], up2),
            (part.at[b, 0, 2, high], relay2.at[b, 1, low], down2),
            (part.at[b, 0, 1, high], got2.at[b, 0, high], up2),
            (part.at[b, 0, 3, low], got2.at[b, 1, low], down2),
            (part.at[b, 0, 1, low], got2.at[b, 0, low], up2),
            (part.at[b, 0, 3, high], got2.at[b, 1, high], down2),
        ]

        def make(m):
            src, dst, who = table[m]
            return remote(src, dst, send_sem, recv_sem, (b, m), "col", who)

        return b, make

    def produce(c, rows):
        where = c % 2 if isinstance(c, int) else lax.rem(c, 2)
        for k in range(2):
            load(c, rows, where, k).wait()
        if isinstance(c, int):
            for k in range(2):
                if c + 1 < STEPS:
                    load(c + 1, ROWS, 1 - where, k).start()
        else:

            @pl.when(c + 1 < STEPS)
            def full():
                for k in range(2):
                    load(c + 1, ROWS, 1 - where, k).start()

            @pl.when(c + 1 == STEPS)
            def short():
                for k in range(2):
                    load(STEPS, last, 1 - where, k).start()

        for k in range(2):
            high, low = split_bf16(staged[where, k, 0:rows])
            lhs[k * rows : (k + 1) * rows] = high
            lhs[(2 + k) * rows : (3 + k) * rows] = low
        trips = [flight(c, rows, k) for k in range(2)]
        for dx in (2, 1, 3, 0):
            if isinstance(c, int) and c == 0:
                mark(dx * SIDE, SIDE)
            out = jnp.dot(
                lhs[0 : 4 * rows], onehot[:, dx * span : (dx + 1) * span], preferred_element_type=jnp.float32
            )
            for k in range(2):
                both = out[k * rows : (k + 1) * rows] + out[(2 + k) * rows : (3 + k) * rows]
                for dz in range(SIDE):
                    piece = both[:, dz * cols : (dz + 1) * cols]
                    if k == 0:
                        part[trips[0][0], dx, dz, 0:rows] = piece
                    else:
                        part[trips[1][0], dz, dx, 0:rows] = piece
            if isinstance(c, int) and c == 0 and dx == 2:
                pl.semaphore_wait(barrier, OWNERS - 1 + groups - 1)
            for m in {2: (0, 1), 1: (2,), 3: (3,), 0: ()}[dx]:
                trips[0][1](m).start()
        for m in range(4):
            trips[1][1](m).start()

    def forward_first(c, rows):
        for k in range(2):
            b, make = flight(c, rows, k)
            make(0).wait_recv()
            part[b, 1, 0:2, 0:rows] = part[b, 1, 0:2, 0:rows] + relay1[b, 0, :, 0:rows]
            make(4).start()
            make(1).wait_recv()
            part[b, 3, 2:4, 0:rows] = part[b, 3, 2:4, 0:rows] + relay1[b, 1, :, 0:rows]
            make(5).start()

    def second_stage(c, rows):
        for k in range(2):
            b, make = flight(c, rows, k)
            for m in (2, 3, 4, 5):
                make(m).wait_recv()
            part[b, 0, :, 0:rows] = part[b, 0, :, 0:rows] + got1[b, 0, :, 0:rows] + got1[b, 1, :, 0:rows]
            for m in (6, 7, 8, 9):
                make(m).start()

    def forward_second(c, rows):
        low = rows // 2
        for k in range(2):
            b, make = flight(c, rows, k)
            make(6).wait_recv()
            part[b, 0, 1, 0:low] = part[b, 0, 1, 0:low] + relay2[b, 0, 0:low]
            make(10).start()
            make(7).wait_recv()
            part[b, 0, 3, low:rows] = part[b, 0, 3, low:rows] + relay2[b, 1, 0:low]
            make(11).start()

    def finish(c, rows):
        for k in range(2):
            b, make = flight(c, rows, k)
            for m in (8, 9, 10, 11):
                make(m).wait_recv()
            at = pl.ds(first_row(c, k), rows)
            right[at] = prior_v[at] + (part[b, 0, 0, 0:rows] + got2[b, 0, 0:rows] + got2[b, 1, 0:rows])
            for m in range(12):
                make(m).wait_send()

    def pack_copy(n):
        dx, dz = n // SIDE, n % SIDE
        return remote(packed.at[n], got_packed.at[n], pack_send, pack_recv, n, "col", col_at(dz, dx))

    def pack_weights():
        numbers = lax.broadcasted_iota(jnp.int32, (OWNERS, cells), 0)
        mine = numbers == owner[...]
        for q in range(cells // 128):
            rows_ = lax.broadcasted_iota(jnp.int32, (128, cells), 0) + q * 128
            before[q * 128 : (q + 1) * 128] = bf16_where(rows_ < lax.broadcasted_iota(jnp.int32, (128, cells), 1))
        counts = jnp.dot(bf16_where(mine), before[...], preferred_element_type=jnp.float32)
        rank = jnp.sum(jnp.where(mine, counts, 0.0), axis=0, keepdims=True)
        place = (block * 128).astype(jnp.float32) + rank
        for n in range(OWNERS):
            packing[n * 128 : (n + 1) * 128] = bf16_where(
                lax.broadcasted_iota(jnp.int32, (128, cells), 0).astype(jnp.float32) + float(n * 128) == place
            )
        high, low = split_bf16(pdf[...])
        slots = jnp.broadcast_to(slot[...].astype(jnp.float32), (bins, cells)).astype(jnp.bfloat16)
        for n in range(OWNERS):
            at = slice(n * 128, (n + 1) * 128)
            out = lax.dot_general(
                jnp.concatenate([high, low, slots], axis=0), packing[at], (((1,), (1,)), ((), ())),
                preferred_element_type=jnp.float32,
            )
            packed[n, 0:bins] = out[0:bins] + out[bins : 2 * bins]
            packed[n, bins : bins + 8] = out[2 * bins : 2 * bins + 8]
        for n in range(1, OWNERS):
            pack_copy(n).start()

    def take_weights():
        got_packed[0] = packed[0]
        for n in range(1, OWNERS):
            pack_copy(n).wait_recv()
        lane = lax.broadcasted_iota(jnp.int32, (cols, 128), 0).astype(jnp.float32)
        for n in range(OWNERS):
            hit = bf16_where(lane == got_packed[n, bins : bins + 1])
            at = slice(n % 2 * 128, (n % 2 + 1) * 128)
            picks[n // 2, 0:cols, at] = hit
            picks[n // 2, cols : 2 * cols, at] = hit

    def split_react():
        react_copy().wait()
        wide_react[...] = jnp.zeros_like(wide_react)
        wide_react[0 : species * bins, 0:species] = react_v[...]

        def one(i, carry):
            high, low = split_bf16(wide_react[pl.ds(i, ROWS, stride=bins)])
            react3[i, :, 0:128] = high
            react3[i, :, 128:256] = low
            react3[i, :, 256:384] = high
            return carry

        lax.fori_loop(0, bins, one, 0)
        solved[...] = jnp.zeros_like(solved)
        right[species * bins :] = jnp.zeros((right.shape[0] - species * bins, cols), jnp.float32)
        edges[groups - 1] = jnp.zeros_like(edges[groups - 1])
        sums[groups - 1] = jnp.zeros_like(sums[groups - 1])

    every_bin = bins * groups

    def pivots(low, high):
        strength = jnp.broadcast_to(dissip[...], (8, cols))

        def one(i, earlier):
            centre = (i.astype(jnp.float32) + 0.5) / every_bin
            diffusion = strength * (4.0 * centre * (1.0 - centre) + 0.05)
            pivot = 1.0 + 2.0 * diffusion - diffusion * earlier
            new = diffusion / pivot
            ratio[i] = new
            inverse[i] = 1.0 / pivot
            return new

        start = jnp.where(low == 0, jnp.zeros((8, cols), jnp.float32), ratio[jnp.maximum(low - 1, 0)])
        lax.fori_loop(low, high, one, start)

    def factors():
        def block_(m, carry):
            def grow(i, g):
                g = g * ratio[m * bins + i]
                grown[m * bins + i] = g
                return g

            lax.fori_loop(0, bins, grow, jnp.ones((8, cols), jnp.float32))

            def shrink(n, both):
                h, d = both
                i = m * bins + bins - 1 - n
                h = grown[i] + ratio[i] * h
                d = ratio[i] * d
                carried[i] = h
                decayed[i] = d
                return h, d

            lax.fori_loop(0, bins, shrink, (jnp.zeros((8, cols), jnp.float32), jnp.ones((8, cols), jnp.float32)))
            return carry

        lax.fori_loop(0, groups, block_, 0)

    def turn(t, carry):
        produce(t, ROWS)
        forward_first(t - 1, ROWS)

        @pl.when(t == 1)
        def _():
            pack_weights()

        pivots((t - 1) * 22, jnp.minimum(t * 22, every_bin))

        @pl.when(t >= 2)
        def _():
            second_stage(t - 2, ROWS)

        @pl.when(t >= 3)
        def _():
            forward_second(t - 3, ROWS)

        @pl.when(t == 3)
        def _():
            prior_copy().wait()

        @pl.when(t >= 4)
        def _():
            finish(t - 4, ROWS)

        return carry

    produce(0, ROWS)
    split_react()
    lax.fori_loop(1, STEPS, turn, 0)
    stages = (produce, forward_first, second_stage, forward_second, finish)
    for t in range(STEPS, STEPS + len(stages)):
        for n, stage in enumerate(stages):
            if n <= t and t - n <= STEPS:
                stage(t - n, last if t - n == STEPS else ROWS)
        if t == STEPS:
            factors()
            take_weights()

    base = bin_ * bins
    value = jnp.zeros((ROWS, cols), jnp.float32)
    for i in range(bins):
        value = right[pl.ds(i, ROWS, stride=bins)] * inverse[base + i, 0:1] + ratio[base + i, 0:1] * value
        lines[i] = value
    for j in range(groups - 1):
        edges[j, 0] = value[16 * j : 16 * j + 16]
    value = jnp.zeros((ROWS, cols), jnp.float32)
    for i in reversed(range(bins)):
        value = lines[i] + ratio[base + i, 0:1] * value
        lines[i] = value
    for j in range(groups - 1):
        edges[j, 1] = value[16 * j : 16 * j + 16]

    def edge_copy(d):
        other = lax.rem(bin_ + d, groups)
        return remote(edges.at[other], got_edges.at[d], edge_send, edge_recv, d, "bin", other)

    for d in range(1, groups):
        edge_copy(d).start()
    got_edges[0] = edges[bin_]
    for d in range(1, groups):
        edge_copy(d).wait_recv()
    value = jnp.zeros((16, cols), jnp.float32)
    for m in range(groups):
        ends[m, 0] = value
        value = got_edges[lax.rem(bin_ - m + groups, groups), 0] + decayed[m * bins, 0:1] * value
    value = jnp.zeros((16, cols), jnp.float32)
    for m in reversed(range(groups)):
        ends[m, 1] = value
        value = (
            got_edges[lax.rem(bin_ - m + groups, groups), 1]
            + carried[m * bins, 0:1] * ends[m, 0]
            + decayed[m * bins, 0:1] * value
        )

    def end_copy(d):
        other = lax.rem(bin_ + d, groups)
        return remote(ends.at[other], got_ends.at[bin_], end_send, end_recv, d, "bin", other)

    def end_arrived(d):
        other = lax.rem(bin_ - d + groups, groups)
        return remote(ends.at[other], got_ends.at[other], end_send, end_recv, d, "bin", other)

    for d in range(1, groups):
        end_copy(d).start()
    got_ends[bin_] = ends[bin_]
    for d in range(1, groups):
        end_arrived(d).wait_recv()
    entering = jnp.concatenate([got_ends[j, 0] for j in range(groups - 1)], axis=0)
    leaving = jnp.concatenate([got_ends[j, 1] for j in range(groups - 1)], axis=0)

    for i in range(bins):
        value = lines[i] + carried[base + i, 0:1] * entering + decayed[base + i, 0:1] * leaving
        high, low = split_bf16(value)
        at = i % 2
        solved[at, 0:ROWS] = high
        solved[at, 128 : 128 + ROWS] = high
        solved[at, 256 : 256 + ROWS] = low
        new = jnp.dot(react3[i], solved[at], preferred_element_type=jnp.float32)
        state[pl.ds(i, species, stride=bins)] = new[0:species]
        high, low = split_bf16(new)
        picked[i * ROWS : (i + 1) * ROWS, 0:cols] = high
        picked[i * ROWS : (i + 1) * ROWS, cols : 2 * cols] = low

    def weigh(n, carry):
        out = jnp.dot(picked[...], picks[n], preferred_element_type=jnp.float32)
        for q in range(2):
            acc = jnp.zeros((ROWS, 128), jnp.float32)
            for i in range(bins):
                acc = acc + out[i * ROWS : (i + 1) * ROWS, q * 128 : (q + 1) * 128] * got_packed[2 * n + q, i : i + 1]
            for j in range(groups - 1):
                sums[j, 2 * n + q] = acc[16 * j : 16 * j + 16]
        return carry

    middle = OWNERS // 2
    parts = (pl.ds(0, middle), pl.ds(middle, middle))

    def twin_copy(dy, h):
        return remote(
            sums.at[bin_at(dy, True), parts[h]], from_twin.at[dy, parts[h]], bin_send, bin_recv, 2 * dy + h, "bin", twin
        )

    y_up, y_down = bin_at(1), bin_at(-1)
    first, rest = parts
    bin_table = [
        (sums.at[bin_at(2), first], relay_b.at[0], y_up),
        (sums.at[bin_at(2), rest], relay_b.at[1], y_down),
        (sums.at[bin_at(1), rest], got_b.at[0, rest], y_up),
        (sums.at[bin_at(3), first], got_b.at[1, first], y_down),
        (sums.at[bin_at(1), first], got_b.at[0, first], y_up),
        (sums.at[bin_at(3), rest], got_b.at[1, rest], y_down),
    ]

    def bin_copy(m):
        src, dst, who = bin_table[m]
        return remote(src, dst, bin_send, bin_recv, 2 * SIDE + m, "bin", who)

    def join_twin(h):
        for dy, m in ((2, h), (3, 3) if h == 0 else (1, 2), (1, None) if h == 0 else (3, None), (0, None)):
            twin_copy(dy, h).wait_recv()
            j = bin_at(dy)
            at = slice(h * middle, (h + 1) * middle)
            sums[j, at] = sums[j, at] + from_twin[dy, at]
            if m is not None:
                bin_copy(m).start()

    lax.fori_loop(0, 4, weigh, 0)
    for dy in (2, 3, 1, 0):
        twin_copy(dy, 0).start()
    lax.fori_loop(4, 6, weigh, 0)
    join_twin(0)
    lax.fori_loop(6, 8, weigh, 0)
    for dy in (2, 1, 3, 0):
        twin_copy(dy, 1).start()
    bin_copy(0).wait_recv()
    sums[bin_at(1), 0:middle] = sums[bin_at(1), 0:middle] + relay_b[0]
    bin_copy(4).start()
    join_twin(1)
    bin_copy(1).wait_recv()
    sums[bin_at(3), middle:OWNERS] = sums[bin_at(3), middle:OWNERS] + relay_b[1]
    bin_copy(5).start()
    for m in (2, 3, 4, 5):
        bin_copy(m).wait_recv()
    total[...] = sums[bin_] + got_b[0] + got_b[1]

    def back_copy(n):
        dx, dz = n // SIDE, n % SIDE
        return remote(total.at[n], back.at[n], back_send, back_recv, n, "col", col_at(-dz, -dx))

    for n in range(1, OWNERS):
        back_copy(n).start()
    back[0] = total[0]
    mine_sum = jnp.zeros((32, cells), jnp.float32)
    for dx in range(SIDE):
        for dz in range(SIDE):
            n = dx * SIDE + dz
            if n:
                back_copy(n).wait_recv()
            high, low = split_bf16(back[n])
            unpacked[dx, 0:16, dz * 128 : (dz + 1) * 128] = high
            unpacked[dx, 16:32, dz * 128 : (dz + 1) * 128] = low
        mine_sum = mine_sum + jnp.dot(
            unpacked[dx], packing[dx * SIDE * 128 : (dx + 1) * SIDE * 128], preferred_element_type=jnp.float32
        )
    gathered[bin_] = mine_sum[0:16] + mine_sum[16:32]

    behind, ahead_, across = bin_at(-1), bin_at(1), bin_at(2)
    top, bottom = pl.ds(0, 8), pl.ds(8, 8)

    near = (bin_at(1), bin_at(1, True), bin_at(-1), bin_at(-1, True), twin)
    halves = (top, bottom)

    def all_copy(m):
        if m < 5:
            ref, who = gathered.at[bin_], near[m]
        else:
            up = m < 7
            ref = gathered.at[behind if up else ahead_, top if up else bottom]
            who = near[m - 5]
        return remote(ref, ref, all_send, all_recv, m, "bin", who)

    def all_arrived(m):
        if m < 5:
            ref = gathered.at[(bin_at(-1), bin_at(-1, True), bin_at(1), bin_at(1, True), twin)[m]]
        else:
            ref = gathered.at[bin_at(2, m % 2 == 0), halves[0] if m < 7 else halves[1]]
        return remote(ref, ref, all_send, all_recv, m, "bin", twin)

    for m in range(5):
        all_copy(m).start()
    all_arrived(0).wait_recv()
    for m in (5, 6):
        all_copy(m).start()
    all_arrived(2).wait_recv()
    for m in (7, 8):
        all_copy(m).start()
    for m in (1, 3, 4, 5, 6, 7, 8):
        all_arrived(m).wait_recv()
    for j in range(groups):
        count = min(16, species - 16 * j)
        if count > 0:
            les[16 * j : 16 * j + count] = gathered[j, 0:count]

    for n in range(1, OWNERS):
        pack_copy(n).wait_send()
        back_copy(n).wait_send()
    for d in range(1, groups):
        edge_copy(d).wait_send()
        end_copy(d).wait_send()
    for dy in range(SIDE):
        for h in range(2):
            twin_copy(dy, h).wait_send()
    for m in range(6):
        bin_copy(m).wait_send()
    for m in range(9):
        all_copy(m).wait_send()


def hand_over(state, les, state_out, les_out, sem):
    pairs = ((state, state_out), (les, les_out))
    copies = [pltpu.make_async_copy(src, dst, sem.at[n]) for n, (src, dst) in enumerate(pairs)]
    for copy in copies:
        copy.start()
    for copy in copies:
        copy.wait()


def local(les_source, cell_owner, cell_slot, pdf_weight, prior_state, dissip, react_inverse):
    bins, species, cells = les_source.shape
    cols = prior_state.shape[2]
    groups = 2 * SIDE
    rows = bins * species
    chunks = 2 * (STEPS + 1)
    f32, bf16 = jnp.float32, jnp.bfloat16

    def by_species(array):
        return jnp.transpose(array, (1, 0, 2)).reshape(rows, array.shape[2])

    vmem, hbm, dma = pl.BlockSpec(memory_space=pltpu.VMEM), pl.BlockSpec(memory_space=pl.ANY), pltpu.SemaphoreType.DMA
    state, les = pl.pallas_call(
        step_kernel,
        out_shape=(jax.ShapeDtypeStruct((rows, cols), f32), jax.ShapeDtypeStruct((species, cells), f32)),
        in_specs=[hbm, vmem, vmem, vmem, hbm, vmem, hbm],
        out_specs=(vmem, vmem),
        scratch_shapes=[
            pltpu.VMEM((2, 2, ROWS, cells), f32),
            pltpu.VMEM((4 * ROWS, cells), bf16),
            pltpu.VMEM((cells, 128), f32),
            pltpu.VMEM((cells, OWNERS * cols), bf16),
            pltpu.VMEM((OWNERS * 128, cells), bf16),
            pltpu.VMEM((cells, cells), bf16),
            pltpu.VMEM((chunks, SIDE, SIDE, ROWS, cols), f32),
            pltpu.VMEM((chunks, 2, 2, ROWS, cols), f32),
            pltpu.VMEM((chunks, 2, SIDE, ROWS, cols), f32),
            pltpu.VMEM((chunks, 2, ROWS // 2, cols), f32),
            pltpu.VMEM((chunks, 2, ROWS, cols), f32),
            pltpu.VMEM((rows, cols), f32),
            pltpu.VMEM((rows, species), f32),
            pltpu.VMEM((ROWS * bins, 128), f32),
            pltpu.VMEM((bins, ROWS, 384), bf16),
            pltpu.VMEM((ROWS * bins, cols), f32),
            pltpu.VMEM((bins * groups, 8, cols), f32),
            pltpu.VMEM((bins * groups, 8, cols), f32),
            pltpu.VMEM((bins * groups, 8, cols), f32),
            pltpu.VMEM((bins * groups, 8, cols), f32),
            pltpu.VMEM((bins * groups, 8, cols), f32),
            pltpu.VMEM((OWNERS, bins + 8, 128), f32),
            pltpu.VMEM((OWNERS, bins + 8, 128), f32),
            pltpu.VMEM((OWNERS // 2, 2 * cols, 256), bf16),
            pltpu.VMEM((bins, ROWS, cols), f32),
            pltpu.VMEM((groups, 2, 16, cols), f32),
            pltpu.VMEM((groups, 2, 16, cols), f32),
            pltpu.VMEM((groups, 2, 16, cols), f32),
            pltpu.VMEM((groups, 2, 16, cols), f32),
            pltpu.VMEM((2, 384, cols), bf16),
            pltpu.VMEM((bins * ROWS, 2 * cols), bf16),
            pltpu.VMEM((groups, OWNERS, 16, 128), f32),
            pltpu.VMEM((SIDE, OWNERS, 16, 128), f32),
            pltpu.VMEM((2, OWNERS // 2, 16, 128), f32),
            pltpu.VMEM((2, OWNERS, 16, 128), f32),
            pltpu.VMEM((OWNERS, 16, 128), f32),
            pltpu.VMEM((OWNERS, 16, 128), f32),
            pltpu.VMEM((SIDE, 32, SIDE * 128), bf16),
            pltpu.VMEM((groups, 16, cells), f32),
            dma((3, 2)),
            dma((chunks, 12)),
            dma((chunks, 12)),
            dma((OWNERS,)),
            dma((OWNERS,)),
            dma((groups,)),
            dma((groups,)),
            dma((groups,)),
            dma((groups,)),
            dma((2 * SIDE + 6,)),
            dma((2 * SIDE + 6,)),
            dma((OWNERS,)),
            dma((OWNERS,)),
            dma((9,)),
            dma((9,)),
        ],
        compiler_params=pltpu.CompilerParams(collective_id=0, has_side_effects=True, vmem_limit_bytes=63 << 20),
        name="cmc_step",
    )(
        by_species(les_source),
        cell_owner.reshape(1, cells),
        cell_slot.reshape(1, cells),
        pdf_weight,
        by_species(prior_state),
        dissip.reshape(1, cols),
        by_species(react_inverse),
    )
    state, les = pl.pallas_call(
        hand_over,
        out_shape=(jax.ShapeDtypeStruct(state.shape, f32), jax.ShapeDtypeStruct(les.shape, f32)),
        in_specs=[hbm, hbm],
        out_specs=(hbm, hbm),
        scratch_shapes=[dma((2,))],
        name="hand_over",
    )(state, les)
    return jnp.transpose(state.reshape(species, bins, cols), (1, 0, 2)), les


def solution(mesh):
    placed = (
        P("bin", None, "col"),
        P("col", None),
        P("col"),
        P("bin", "col"),
        P("bin", None, "col"),
        P("col"),
        P("bin", None, None),
    )
    return jax.shard_map(
        local,
        mesh=mesh,
        in_specs=placed,
        out_specs=(P("bin", None, "col"), P(None, "col")),
        check_vma=False,
    )
```

```python
import jax
import jax.numpy as jnp
from jax import lax
from jax.experimental import pallas as pl
from jax.experimental.pallas import tpu as pltpu
from jax.sharding import PartitionSpec as P

SIDE = 4
OWNERS = SIDE * SIDE
ROWS = 112
STEPS = 7
MESH = pl.DeviceIdType.MESH


def split_bf16(value):
    high = value.astype(jnp.bfloat16)
    return high, (value - high.astype(jnp.float32)).astype(jnp.bfloat16)


def bf16_where(mask):
    return mask.astype(jnp.float32).astype(jnp.bfloat16)


def step_kernel(
    source, owner, slot, pdf, prior, dissip, react,
    state, les,
    staged, lhs, tall, onehot, packing, before, part, relay1, got1, relay2, got2,
    prior_v, react_v, wide_react, react3, right, ratio, inverse, grown, carried, decayed,
    packed, got_packed, picks, lines, edges, got_edges, ends, got_ends, solved, picked,
    sums, from_twin, relay_b, got_b, total, back, unpacked, gathered,
    load_sem, send_sem, recv_sem, pack_send, pack_recv, edge_send, edge_recv, end_send, end_recv,
    bin_send, bin_recv, back_send, back_recv, all_send, all_recv,
):
    cells = source.shape[1]
    cols = prior.shape[1]
    bins = pdf.shape[0]
    species = prior.shape[0] // bins
    half = prior.shape[0] // 2
    last = half - STEPS * ROWS
    span = SIDE * cols
    padded = solved.shape[1]
    col, bin_ = lax.axis_index("col"), lax.axis_index("bin")
    z, x = col // SIDE, lax.rem(col, SIDE)
    y, core = bin_ // 2, lax.rem(bin_, 2)
    groups = 2 * SIDE

    def col_at(dz, dx):
        return lax.rem(z + dz + SIDE, SIDE) * SIDE + lax.rem(x + dx + SIDE, SIDE)

    def bin_at(dy, other=False):
        return lax.rem(y + dy + SIDE, SIDE) * 2 + (1 - core if other else core)

    x_up, x_down, z_up, z_down = col_at(0, 1), col_at(0, -1), col_at(1, 0), col_at(-1, 0)
    twin = bin_at(0, True)

    def remote(src, dst, sends, recvs, at, axis, who):
        return pltpu.make_async_remote_copy(
            src_ref=src, dst_ref=dst, send_sem=sends.at[at], recv_sem=recvs.at[at],
            device_id={axis: who}, device_id_type=MESH,
        )

    def first_row(c, k):
        return pl.multiple_of(c * ROWS + k * half, 8)

    def load(c, rows, where, k):
        return pltpu.make_async_copy(
            source.at[pl.ds(first_row(c, k), rows)], staged.at[where, k, pl.ds(0, rows)], load_sem.at[where, k]
        )

    def prior_copy():
        return pltpu.make_async_copy(prior, prior_v, load_sem.at[2, 0])

    def react_copy():
        return pltpu.make_async_copy(react, react_v, load_sem.at[2, 1])

    for k in range(2):
        load(0, ROWS, 0, k).start()
    react_copy().start()
    prior_copy().start()
    barrier = pltpu.get_barrier_semaphore()
    for dx in range(SIDE):
        for dz in range(SIDE):
            if dx or dz:
                pl.semaphore_signal(barrier, inc=1, device_id={"col": col_at(dz, dx)}, device_id_type=MESH)
    for d in range(1, groups):
        pl.semaphore_signal(barrier, inc=1, device_id={"bin": lax.rem(bin_ + d, groups)}, device_id_type=MESH)

    ahead = ((owner[...] & (SIDE - 1)) - x) & (SIDE - 1)
    block = ahead * SIDE + (((owner[...] >> 2) - z) & (SIDE - 1))

    relative = (block * cols + slot[...]).astype(jnp.float32)
    for q in range(cells // 128):
        at_q = slice(q * 128, (q + 1) * 128)
        tall[at_q] = jnp.transpose(jnp.broadcast_to(relative[:, at_q], (128, 128)))

    def mark(first, count):
        lane = lax.broadcasted_iota(jnp.int32, (128, 128), 1).astype(jnp.float32)
        for q in range(cells // 128):
            at_q = slice(q * 128, (q + 1) * 128)
            for n in range(first, first + count):
                onehot[at_q, n * 128 : (n + 1) * 128] = bf16_where(tall[at_q] == lane + float(n * 128))

    ways_of = ((x_up, x_down, z_up, z_down), (z_up, z_down, x_up, x_down))

    def flight(c, rows, k):
        b = c + k * (STEPS + 1)
        up1, down1, up2, down2 = ways_of[k]
        every, low, high = pl.ds(0, rows), pl.ds(0, rows // 2), pl.ds(rows // 2, rows // 2)
        first, rest = pl.ds(0, 2), pl.ds(2, 2)
        table = [
            (part.at[b, 2, first, every], relay1.at[b, 0, :, every], up1),
            (part.at[b, 2, rest, every], relay1.at[b, 1, :, every], down1),
            (part.at[b, 1, rest, every], got1.at[b, 0, rest, every], up1),
            (part.at[b, 3, first, every], got1.at[b, 1, first, every], down1),
            (part.at[b, 1, first, every], got1.at[b, 0, first, every], up1),
            (part.at[b, 3, rest, every], got1.at[b, 1, rest, every], down1),
            (part.at[b, 0, 2, low], relay2.at[b, 0, low], up2),
            (part.at[b, 0, 2, high], relay2.at[b, 1, low], down2),
            (part.at[b, 0, 1, high], got2.at[b, 0, high], up2),
            (part.at[b, 0, 3, low], got2.at[b, 1, low], down2),
            (part.at[b, 0, 1, low], got2.at[b, 0, low], up2),
            (part.at[b, 0, 3, high], got2.at[b, 1, high], down2),
        ]

        def make(m):
            src, dst, who = table[m]
            return remote(src, dst, send_sem, recv_sem, (b, m), "col", who)

        return b, make

    def produce(c, rows):
        where = c % 2 if isinstance(c, int) else lax.rem(c, 2)
        for k in range(2):
            load(c, rows, where, k).wait()
        if isinstance(c, int):
            for k in range(2):
                if c + 1 < STEPS:
                    load(c + 1, ROWS, 1 - where, k).start()
        else:

            @pl.when(c + 1 < STEPS)
            def full():
                for k in range(2):
                    load(c + 1, ROWS, 1 - where, k).start()

            @pl.when(c + 1 == STEPS)
            def short():
                for k in range(2):
                    load(STEPS, last, 1 - where, k).start()

        for k in range(2):
            high, low = split_bf16(staged[where, k, 0:rows])
            lhs[k * rows : (k + 1) * rows] = high
            lhs[(2 + k) * rows : (3 + k) * rows] = low
        trips = [flight(c, rows, k) for k in range(2)]
        for dx in (2, 1, 3, 0):
            if isinstance(c, int) and c == 0:
                mark(dx * SIDE, SIDE)
            out = jnp.dot(
                lhs[0 : 4 * rows], onehot[:, dx * span : (dx + 1) * span], preferred_element_type=jnp.float32
            )
            for k in range(2):
                both = out[k * rows : (k + 1) * rows] + out[(2 + k) * rows : (3 + k) * rows]
                for dz in range(SIDE):
                    piece = both[:, dz * cols : (dz + 1) * cols]
                    if k == 0:
                        part[trips[0][0], dx, dz, 0:rows] = piece
                    else:
                        part[trips[1][0], dz, dx, 0:rows] = piece
            if isinstance(c, int) and c == 0 and dx == 2:
                pl.semaphore_wait(barrier, OWNERS - 1 + groups - 1)
            for m in {2: (0, 1), 1: (2,), 3: (3,), 0: ()}[dx]:
                trips[0][1](m).start()
        for m in range(4):
            trips[1][1](m).start()

    def forward_first(c, rows):
        for k in range(2):
            b, make = flight(c, rows, k)
            make(0).wait_recv()
            part[b, 1, 0:2, 0:rows] = part[b, 1, 0:2, 0:rows] + relay1[b, 0, :, 0:rows]
            make(4).start()
            make(1).wait_recv()
            part[b, 3, 2:4, 0:rows] = part[b, 3, 2:4, 0:rows] + relay1[b, 1, :, 0:rows]
            make(5).start()

    def second_stage(c, rows):
        for k in range(2):
            b, make = flight(c, rows, k)
            for m in (2, 3, 4, 5):
                make(m).wait_recv()
            part[b, 0, :, 0:rows] = part[b, 0, :, 0:rows] + got1[b, 0, :, 0:rows] + got1[b, 1, :, 0:rows]
            for m in (6, 7, 8, 9):
                make(m).start()

    def forward_second(c, rows):
        low = rows // 2
        for k in range(2):
            b, make = flight(c, rows, k)
            make(6).wait_recv()
            part[b, 0, 1, 0:low] = part[b, 0, 1, 0:low] + relay2[b, 0, 0:low]
            make(10).start()
            make(7).wait_recv()
            part[b, 0, 3, low:rows] = part[b, 0, 3, low:rows] + relay2[b, 1, 0:low]
            make(11).start()

    def finish(c, rows):
        for k in range(2):
            b, make = flight(c, rows, k)
            for m in (8, 9, 10, 11):
                make(m).wait_recv()
            at = pl.ds(first_row(c, k), rows)
            right[at] = prior_v[at] + (part[b, 0, 0, 0:rows] + got2[b, 0, 0:rows] + got2[b, 1, 0:rows])
            for m in range(12):
                make(m).wait_send()

    def pack_copy(n):
        dx, dz = n // SIDE, n % SIDE
        return remote(packed.at[n], got_packed.at[n], pack_send, pack_recv, n, "col", col_at(dz, dx))

    def pack_weights():
        numbers = lax.broadcasted_iota(jnp.int32, (OWNERS, cells), 0)
        mine = numbers == owner[...]
        for q in range(cells // 128):
            rows_ = lax.broadcasted_iota(jnp.int32, (128, cells), 0) + q * 128
            before[q * 128 : (q + 1) * 128] = bf16_where(rows_ < lax.broadcasted_iota(jnp.int32, (128, cells), 1))
        counts = jnp.dot(bf16_where(mine), before[...], preferred_element_type=jnp.float32)
        rank = jnp.sum(jnp.where(mine, counts, 0.0), axis=0, keepdims=True)
        place = (block * 128).astype(jnp.float32) + rank
        for n in range(OWNERS):
            packing[n * 128 : (n + 1) * 128] = bf16_where(
                lax.broadcasted_iota(jnp.int32, (128, cells), 0).astype(jnp.float32) + float(n * 128) == place
            )
        high, low = split_bf16(pdf[...])
        slots = jnp.broadcast_to(slot[...].astype(jnp.float32), (bins, cells)).astype(jnp.bfloat16)
        for n in range(OWNERS):
            at = slice(n * 128, (n + 1) * 128)
            out = lax.dot_general(
                jnp.concatenate([high, low, slots], axis=0), packing[at], (((1,), (1,)), ((), ())),
                preferred_element_type=jnp.float32,
            )
            packed[n, 0:bins] = out[0:bins] + out[bins : 2 * bins]
            packed[n, bins : bins + 8] = out[2 * bins : 2 * bins + 8]
        for n in range(1, OWNERS):
            pack_copy(n).start()

    def take_weights():
        got_packed[0] = packed[0]
        for n in range(1, OWNERS):
            pack_copy(n).wait_recv()
        lane = lax.broadcasted_iota(jnp.int32, (cols, 128), 0).astype(jnp.float32)
        for n in range(OWNERS):
            hit = bf16_where(lane == got_packed[n, bins : bins + 1])
            at = slice(n % 2 * 128, (n % 2 + 1) * 128)
            picks[n // 2, 0:cols, at] = hit
            picks[n // 2, cols : 2 * cols, at] = hit

    def split_react():
        react_copy().wait()
        wide_react[...] = jnp.zeros_like(wide_react)
        wide_react[0 : species * bins, 0:species] = react_v[...]

        def one(i, carry):
            high, low = split_bf16(wide_react[pl.ds(i, ROWS, stride=bins)])
            react3[i, :, 0:128] = high
            react3[i, :, 128:256] = low
            react3[i, :, 256:384] = high
            return carry

        lax.fori_loop(0, bins, one, 0)
        solved[...] = jnp.zeros_like(solved)
        right[species * bins :] = jnp.zeros((right.shape[0] - species * bins, cols), jnp.float32)
        edges[groups - 1] = jnp.zeros_like(edges[groups - 1])
        sums[groups - 1] = jnp.zeros_like(sums[groups - 1])

    every_bin = bins * groups

    def pivots(low, high):
        strength = jnp.broadcast_to(dissip[...], (8, cols))

        def one(i, earlier):
            centre = (i.astype(jnp.float32) + 0.5) / every_bin
            diffusion = strength * (4.0 * centre * (1.0 - centre) + 0.05)
            pivot = 1.0 + 2.0 * diffusion - diffusion * earlier
            new = diffusion / pivot
            ratio[i] = new
            inverse[i] = 1.0 / pivot
            return new

        start = jnp.where(low == 0, jnp.zeros((8, cols), jnp.float32), ratio[jnp.maximum(low - 1, 0)])
        lax.fori_loop(low, high, one, start)

    def factors():
        def block_(m, carry):
            def grow(i, g):
                g = g * ratio[m * bins + i]
                grown[m * bins + i] = g
                return g

            lax.fori_loop(0, bins, grow, jnp.ones((8, cols), jnp.float32))

            def shrink(n, both):
                h, d = both
                i = m * bins + bins - 1 - n
                h = grown[i] + ratio[i] * h
                d = ratio[i] * d
                carried[i] = h
                decayed[i] = d
                return h, d

            lax.fori_loop(0, bins, shrink, (jnp.zeros((8, cols), jnp.float32), jnp.ones((8, cols), jnp.float32)))
            return carry

        lax.fori_loop(0, groups, block_, 0)

    def turn(t, carry):
        produce(t, ROWS)
        forward_first(t - 1, ROWS)

        @pl.when(t == 1)
        def _():
            pack_weights()

        pivots((t - 1) * 22, jnp.minimum(t * 22, every_bin))

        @pl.when(t >= 2)
        def _():
            second_stage(t - 2, ROWS)

        @pl.when(t >= 3)
        def _():
            forward_second(t - 3, ROWS)

        @pl.when(t == 3)
        def _():
            prior_copy().wait()

        @pl.when(t >= 4)
        def _():
            finish(t - 4, ROWS)

        return carry

    produce(0, ROWS)
    split_react()
    lax.fori_loop(1, STEPS, turn, 0)
    stages = (produce, forward_first, second_stage, forward_second, finish)
    for t in range(STEPS, STEPS + len(stages)):
        for n, stage in enumerate(stages):
            if n <= t and t - n <= STEPS:
                stage(t - n, last if t - n == STEPS else ROWS)
        if t == STEPS:
            factors()
            take_weights()

    base = bin_ * bins
    value = jnp.zeros((ROWS, cols), jnp.float32)
    for i in range(bins):
        value = right[pl.ds(i, ROWS, stride=bins)] * inverse[base + i, 0:1] + ratio[base + i, 0:1] * value
        lines[i] = value
    for j in range(groups - 1):
        edges[j, 0] = value[16 * j : 16 * j + 16]
    value = jnp.zeros((ROWS, cols), jnp.float32)
    for i in reversed(range(bins)):
        value = lines[i] + ratio[base + i, 0:1] * value
        lines[i] = value
    for j in range(groups - 1):
        edges[j, 1] = value[16 * j : 16 * j + 16]

    def edge_copy(d):
        other = lax.rem(bin_ + d, groups)
        return remote(edges.at[other], got_edges.at[d], edge_send, edge_recv, d, "bin", other)

    for d in range(1, groups):
        edge_copy(d).start()
    got_edges[0] = edges[bin_]
    for d in range(1, groups):
        edge_copy(d).wait_recv()
    value = jnp.zeros((16, cols), jnp.float32)
    for m in range(groups):
        ends[m, 0] = value
        value = got_edges[lax.rem(bin_ - m + groups, groups), 0] + decayed[m * bins, 0:1] * value
    value = jnp.zeros((16, cols), jnp.float32)
    for m in reversed(range(groups)):
        ends[m, 1] = value
        value = (
            got_edges[lax.rem(bin_ - m + groups, groups), 1]
            + carried[m * bins, 0:1] * ends[m, 0]
            + decayed[m * bins, 0:1] * value
        )

    def end_copy(d):
        other = lax.rem(bin_ + d, groups)
        return remote(ends.at[other], got_ends.at[bin_], end_send, end_recv, d, "bin", other)

    def end_arrived(d):
        other = lax.rem(bin_ - d + groups, groups)
        return remote(ends.at[other], got_ends.at[other], end_send, end_recv, d, "bin", other)

    for d in range(1, groups):
        end_copy(d).start()
    got_ends[bin_] = ends[bin_]
    for d in range(1, groups):
        end_arrived(d).wait_recv()
    entering = jnp.concatenate([got_ends[j, 0] for j in range(groups - 1)], axis=0)
    leaving = jnp.concatenate([got_ends[j, 1] for j in range(groups - 1)], axis=0)

    for i in range(bins):
        value = lines[i] + carried[base + i, 0:1] * entering + decayed[base + i, 0:1] * leaving
        high, low = split_bf16(value)
        at = i % 2
        solved[at, 0:ROWS] = high
        solved[at, 128 : 128 + ROWS] = high
        solved[at, 256 : 256 + ROWS] = low
        new = jnp.dot(react3[i], solved[at], preferred_element_type=jnp.float32)
        state[pl.ds(i, species, stride=bins)] = new[0:species]
        high, low = split_bf16(new)
        picked[i * ROWS : (i + 1) * ROWS, 0:cols] = high
        picked[i * ROWS : (i + 1) * ROWS, cols : 2 * cols] = low

    def weigh(n, carry):
        out = jnp.dot(picked[...], picks[n], preferred_element_type=jnp.float32)
        for q in range(2):
            acc = jnp.zeros((ROWS, 128), jnp.float32)
            for i in range(bins):
                acc = acc + out[i * ROWS : (i + 1) * ROWS, q * 128 : (q + 1) * 128] * got_packed[2 * n + q, i : i + 1]
            for j in range(groups - 1):
                sums[j, 2 * n + q] = acc[16 * j : 16 * j + 16]
        return carry

    middle = OWNERS // 2
    parts = (pl.ds(0, middle), pl.ds(middle, middle))

    def twin_copy(dy, h):
        return remote(
            sums.at[bin_at(dy, True), parts[h]], from_twin.at[dy, parts[h]], bin_send, bin_recv, 2 * dy + h, "bin", twin
        )

    y_up, y_down = bin_at(1), bin_at(-1)
    first, rest = parts
    bin_table = [
        (sums.at[bin_at(2), first], relay_b.at[0], y_up),
        (sums.at[bin_at(2), rest], relay_b.at[1], y_down),
        (sums.at[bin_at(1), rest], got_b.at[0, rest], y_up),
        (sums.at[bin_at(3), first], got_b.at[1, first], y_down),
        (sums.at[bin_at(1), first], got_b.at[0, first], y_up),
        (sums.at[bin_at(3), rest], got_b.at[1, rest], y_down),
    ]

    def bin_copy(m):
        src, dst, who = bin_table[m]
        return remote(src, dst, bin_send, bin_recv, 2 * SIDE + m, "bin", who)

    def join_twin(h):
        for dy, m in ((2, h), (3, 3) if h == 0 else (1, 2), (1, None) if h == 0 else (3, None), (0, None)):
            twin_copy(dy, h).wait_recv()
            j = bin_at(dy)
            at = slice(h * middle, (h + 1) * middle)
            sums[j, at] = sums[j, at] + from_twin[dy, at]
            if m is not None:
                bin_copy(m).start()

    lax.fori_loop(0, 4, weigh, 0)
    for dy in (2, 3, 1, 0):
        twin_copy(dy, 0).start()
    lax.fori_loop(4, 6, weigh, 0)
    join_twin(0)
    lax.fori_loop(6, 8, weigh, 0)
    for dy in (2, 1, 3, 0):
        twin_copy(dy, 1).start()
    bin_copy(0).wait_recv()
    sums[bin_at(1), 0:middle] = sums[bin_at(1), 0:middle] + relay_b[0]
    bin_copy(4).start()
    join_twin(1)
    bin_copy(1).wait_recv()
    sums[bin_at(3), middle:OWNERS] = sums[bin_at(3), middle:OWNERS] + relay_b[1]
    bin_copy(5).start()
    for m in (2, 3, 4, 5):
        bin_copy(m).wait_recv()
    total[...] = sums[bin_] + got_b[0] + got_b[1]

    def back_copy(n):
        dx, dz = n // SIDE, n % SIDE
        return remote(total.at[n], back.at[n], back_send, back_recv, n, "col", col_at(-dz, -dx))

    for n in range(1, OWNERS):
        back_copy(n).start()
    back[0] = total[0]
    mine_sum = jnp.zeros((32, cells), jnp.float32)
    for dx in range(SIDE):
        for dz in range(SIDE):
            n = dx * SIDE + dz
            if n:
                back_copy(n).wait_recv()
            high, low = split_bf16(back[n])
            unpacked[dx, 0:16, dz * 128 : (dz + 1) * 128] = high
            unpacked[dx, 16:32, dz * 128 : (dz + 1) * 128] = low
        mine_sum = mine_sum + jnp.dot(
            unpacked[dx], packing[dx * SIDE * 128 : (dx + 1) * SIDE * 128], preferred_element_type=jnp.float32
        )
    gathered[bin_] = mine_sum[0:16] + mine_sum[16:32]

    behind, ahead_, across = bin_at(-1), bin_at(1), bin_at(2)
    top, bottom = pl.ds(0, 8), pl.ds(8, 8)

    near = (bin_at(1), bin_at(1, True), bin_at(-1), bin_at(-1, True), twin)
    halves = (top, bottom)

    def all_copy(m):
        if m < 5:
            ref, who = gathered.at[bin_], near[m]
        else:
            up = m < 7
            ref = gathered.at[behind if up else ahead_, top if up else bottom]
            who = near[m - 5]
        return remote(ref, ref, all_send, all_recv, m, "bin", who)

    def all_arrived(m):
        if m < 5:
            ref = gathered.at[(bin_at(-1), bin_at(-1, True), bin_at(1), bin_at(1, True), twin)[m]]
        else:
            ref = gathered.at[bin_at(2, m % 2 == 0), halves[0] if m < 7 else halves[1]]
        return remote(ref, ref, all_send, all_recv, m, "bin", twin)

    for m in range(5):
        all_copy(m).start()
    all_arrived(0).wait_recv()
    for m in (5, 6):
        all_copy(m).start()
    all_arrived(2).wait_recv()
    for m in (7, 8):
        all_copy(m).start()
    for m in (1, 3, 4, 5, 6, 7, 8):
        all_arrived(m).wait_recv()
    for j in range(groups):
        count = min(16, species - 16 * j)
        if count > 0:
            les[16 * j : 16 * j + count] = gathered[j, 0:count]

    for n in range(1, OWNERS):
        pack_copy(n).wait_send()
        back_copy(n).wait_send()
    for d in range(1, groups):
        edge_copy(d).wait_send()
        end_copy(d).wait_send()
    for dy in range(SIDE):
        for h in range(2):
            twin_copy(dy, h).wait_send()
    for m in range(6):
        bin_copy(m).wait_send()
    for m in range(9):
        all_copy(m).wait_send()


def hand_over(state, les, state_out, les_out):
    state_out[...] = state[...]
    les_out[...] = les[...]


def local(les_source, cell_owner, cell_slot, pdf_weight, prior_state, dissip, react_inverse):
    bins, species, cells = les_source.shape
    cols = prior_state.shape[2]
    groups = 2 * SIDE
    rows = bins * species
    chunks = 2 * (STEPS + 1)
    f32, bf16 = jnp.float32, jnp.bfloat16

    def by_species(array):
        return jnp.transpose(array, (1, 0, 2)).reshape(rows, array.shape[2])

    vmem, hbm, dma = pl.BlockSpec(memory_space=pltpu.VMEM), pl.BlockSpec(memory_space=pl.ANY), pltpu.SemaphoreType.DMA
    state, les = pl.pallas_call(
        step_kernel,
        out_shape=(jax.ShapeDtypeStruct((rows, cols), f32), jax.ShapeDtypeStruct((species, cells), f32)),
        in_specs=[hbm, vmem, vmem, vmem, hbm, vmem, hbm],
        out_specs=(vmem, vmem),
        scratch_shapes=[
            pltpu.VMEM((2, 2, ROWS, cells), f32),
            pltpu.VMEM((4 * ROWS, cells), bf16),
            pltpu.VMEM((cells, 128), f32),
            pltpu.VMEM((cells, OWNERS * cols), bf16),
            pltpu.VMEM((OWNERS * 128, cells), bf16),
            pltpu.VMEM((cells, cells), bf16),
            pltpu.VMEM((chunks, SIDE, SIDE, ROWS, cols), f32),
            pltpu.VMEM((chunks, 2, 2, ROWS, cols), f32),
            pltpu.VMEM((chunks, 2, SIDE, ROWS, cols), f32),
            pltpu.VMEM((chunks, 2, ROWS // 2, cols), f32),
            pltpu.VMEM((chunks, 2, ROWS, cols), f32),
            pltpu.VMEM((rows, cols), f32),
            pltpu.VMEM((rows, species), f32),
            pltpu.VMEM((ROWS * bins, 128), f32),
            pltpu.VMEM((bins, ROWS, 384), bf16),
            pltpu.VMEM((ROWS * bins, cols), f32),
            pltpu.VMEM((bins * groups, 8, cols), f32),
            pltpu.VMEM((bins * groups, 8, cols), f32),
            pltpu.VMEM((bins * groups, 8, cols), f32),
            pltpu.VMEM((bins * groups, 8, cols), f32),
            pltpu.VMEM((bins * groups, 8, cols), f32),
            pltpu.VMEM((OWNERS, bins + 8, 128), f32),
            pltpu.VMEM((OWNERS, bins + 8, 128), f32),
            pltpu.VMEM((OWNERS // 2, 2 * cols, 256), bf16),
            pltpu.VMEM((bins, ROWS, cols), f32),
            pltpu.VMEM((groups, 2, 16, cols), f32),
            pltpu.VMEM((groups, 2, 16, cols), f32),
            pltpu.VMEM((groups, 2, 16, cols), f32),
            pltpu.VMEM((groups, 2, 16, cols), f32),
            pltpu.VMEM((2, 384, cols), bf16),
            pltpu.VMEM((bins * ROWS, 2 * cols), bf16),
            pltpu.VMEM((groups, OWNERS, 16, 128), f32),
            pltpu.VMEM((SIDE, OWNERS, 16, 128), f32),
            pltpu.VMEM((2, OWNERS // 2, 16, 128), f32),
            pltpu.VMEM((2, OWNERS, 16, 128), f32),
            pltpu.VMEM((OWNERS, 16, 128), f32),
            pltpu.VMEM((OWNERS, 16, 128), f32),
            pltpu.VMEM((SIDE, 32, SIDE * 128), bf16),
            pltpu.VMEM((groups, 16, cells), f32),
            dma((3, 2)),
            dma((chunks, 12)),
            dma((chunks, 12)),
            dma((OWNERS,)),
            dma((OWNERS,)),
            dma((groups,)),
            dma((groups,)),
            dma((groups,)),
            dma((groups,)),
            dma((2 * SIDE + 6,)),
            dma((2 * SIDE + 6,)),
            dma((OWNERS,)),
            dma((OWNERS,)),
            dma((9,)),
            dma((9,)),
        ],
        compiler_params=pltpu.CompilerParams(collective_id=0, has_side_effects=True, vmem_limit_bytes=63 << 20),
        name="cmc_step",
    )(
        by_species(les_source),
        cell_owner.reshape(1, cells),
        cell_slot.reshape(1, cells),
        pdf_weight,
        by_species(prior_state),
        dissip.reshape(1, cols),
        by_species(react_inverse),
    )
    state, les = pl.pallas_call(
        hand_over,
        out_shape=(jax.ShapeDtypeStruct(state.shape, f32), jax.ShapeDtypeStruct(les.shape, f32)),
        in_specs=[vmem, vmem],
        out_specs=(vmem, vmem),
        compiler_params=pltpu.CompilerParams(vmem_limit_bytes=8 << 20),
        name="hand_over",
    )(state, les)
    return jnp.transpose(state.reshape(species, bins, cols), (1, 0, 2)), les


def solution(mesh):
    placed = (
        P("bin", None, "col"),
        P("col", None),
        P("col"),
        P("bin", "col"),
        P("bin", None, "col"),
        P("col"),
        P("bin", None, None),
    )
    return jax.shard_map(
        local,
        mesh=mesh,
        in_specs=placed,
        out_specs=(P("bin", None, "col"), P(None, "col")),
        check_vma=False,
    )
```
